32 devices in a mesh: dp: 8 (over z, y), group: 4 (over x, core).
Axes of the slice: x: 2, y: 2, z: 4, core: 2. Of those that a mesh axis runs over, the one named last changes fastest.
Arguments:
- gradients: float32 [32, 3, 320, 960], P(('dp', 'group')), may hold values from -0.8 to 0.8
- errors: bfloat16 [32, 3, 320, 960], P(('dp', 'group')), may hold values from -0.59765625 to 0.59765625
- q_init: float32 [3, 960, 32], replicated, may hold values from -0.1875 to 0.1875
- owners: int32 [3], replicated, may hold values from 0 to 31, as said below
- buckets: int32 [3], replicated, may hold values from 0 to 3
- learn_rates: float32 [4], replicated, may hold values from 0.2 to 1
- beta_values: float32 [4], replicated, may hold values from 0.5 to 0.95
- momentum: bfloat16 [64, 320, 960], P(('dp', 'group')), may hold values from -3 to 3
Outputs:
- new_errors: bfloat16 [32, 3, 320, 960], P(('dp', 'group'))
- weight_steps: bfloat16 [32, 3, 320, 960], P(('dp', 'group'))
- new_momentum: bfloat16 [64, 320, 960], P(('dp', 'group'))
The draws below stay inside these ranges and needn't reach their ends.
Inputs may be any that keep to these rules, and one draw needn't show every extreme that they name: `owners`: no device owns more than 2 matrices, and some device owns exactly 2.
All inputs are finite; a program needn't handle non-finite values.
Results may differ from the reference program's by a relative error of at most 0.001.
Values may be sent and summed in bfloat16 or wider, within the bound.
No kernel may reach another device: no remote copies, remote signals or barrier semaphores. Data moves between devices by JAX's collectives and lax.ppermute only.
A program may use at most 64 MiB of HBM per device.

```python
import math
import jax
import jax.numpy as jnp
from jax import lax

D = 960
DKV = 320
RANK = 32
MATS = 3
SLOTS = 2
BUCKETS = 4
DEVICES = 32


def draw_gradients(key, part):
    first = jax.random.fold_in(key, 0)
    shape = (DEVICES, MATS, DKV, D)
    values = jax.random.normal(first, shape, jnp.float32) * 0.1
    return jnp.clip(values, -0.8, 0.8)


def draw_owners(key, part):
    first, second, third = jax.random.split(jax.random.fold_in(key, 17), 3)
    doubled = jax.random.randint(first, (), 0, DEVICES)
    single = (doubled + jax.random.randint(second, (), 1, DEVICES)) % DEVICES
    position = jax.random.randint(third, (), 0, MATS)
    index = jnp.arange(MATS, dtype=jnp.int32)
    return jnp.where(index == position, single, doubled).astype(jnp.int32)


def shard_levels(own_key, dims, cuts, smallest, high):
    def one(dim, shards_of):
        draws = jax.random.uniform(jax.random.fold_in(jax.random.fold_in(own_key, 6), dim), (shards_of,), jnp.float32, smallest / len(cuts), high / len(cuts))
        return jnp.repeat(jnp.exp(draws), dims[dim] // shards_of).reshape((-1,) + (1,) * (len(dims) - dim - 1))

    factor_of = one(*cuts[0])
    for cut in cuts[1:]:
        factor_of = factor_of * one(*cut)
    return factor_of


def scatter_about(stream_key, shape, spread, limit, shards=(), kind=jnp.bfloat16):
    gain = shard_levels(stream_key, shape, shards, -0.22, 0.18) if shards else 1.0
    drawn = jax.random.normal(stream_key, shape, jnp.float32) * spread * gain
    return jnp.minimum(jnp.maximum(drawn, -limit), limit).astype(kind)


def setup_inputs(seed: int = 0) -> dict:
    streams_of = jax.random.split(jax.random.key(seed), 9)
    return {
        "gradients": draw_gradients(jax.random.fold_in(streams_of[8], 71), 0),
        "errors": scatter_about(streams_of[1], (DEVICES, MATS, DKV, D), 0.1, 0.59765625, ((0, 32),)),
        "q_init": scatter_about(streams_of[2], (MATS, D, RANK), D ** -0.5, 0.1875, (), jnp.float32),
        "owners": draw_owners(jax.random.fold_in(streams_of[8], 71), 0),
        "buckets": jax.random.randint(streams_of[4], (MATS,), 0, BUCKETS).astype(jnp.int32),
        "learn_rates": jnp.clip(jnp.exp(jax.random.uniform(streams_of[5], (BUCKETS,), jnp.float32, math.log(0.2), math.log(1.0))), 0.2, 1.0),
        "beta_values": jnp.clip(jax.random.uniform(streams_of[6], (BUCKETS,), jnp.float32, 0.5, 0.95), 0.5, 0.95),
        "momentum": scatter_about(streams_of[7], (DEVICES * SLOTS, DKV, D), 0.5, 3.0, ((0, 32),)),
    }


def reference(gradients, errors, q_init, owners, buckets, learn_rates, beta_values, momentum):
    highest = lax.Precision.HIGHEST

    def add_left(total, pair):
        grad_part, error_part = pair
        merged = grad_part + error_part.astype(jnp.float32)
        return (total + jnp.einsum('mkd,mdr->mkr', merged, q_init, precision=highest), None)
    p_sum, _ = lax.scan(add_left, jnp.zeros((MATS, DKV, RANK), jnp.float32), (gradients, errors))
    gram_matrix = jnp.einsum('mkr,mks->mrs', p_sum, p_sum, precision=highest)
    lower_factor = jnp.linalg.cholesky(gram_matrix)
    p_hat = lax.linalg.triangular_solve(lower_factor, p_sum, left_side=False, lower=True, transpose_a=True)

    def add_right(total, pair):
        grad_part, error_part = pair
        merged = grad_part + error_part.astype(jnp.float32)
        q_local = jnp.einsum('mkd,mkr->mdr', merged, p_hat, precision=highest)
        approx = jnp.einsum('mkr,mdr->mkd', p_hat, q_local, precision=highest)
        return (total + q_local, (merged - approx).astype(jnp.bfloat16))
    q_sum, new_errors = lax.scan(add_right, jnp.zeros((MATS, D, RANK), jnp.float32), (gradients, errors))
    update = jnp.einsum('mkr,mdr->mkd', p_hat, q_sum, precision=highest)
    positions = jnp.arange(MATS, dtype=jnp.int32)
    earlier = (owners[None, :] == owners[:, None]) & (positions[None, :] < positions[:, None])
    slot_list = jnp.sum(earlier.astype(jnp.int32), axis=1).astype(jnp.int32)
    flat_index = (owners * SLOTS + slot_list).astype(jnp.int32)
    old_state = momentum[flat_index].astype(jnp.float32)
    rate_list = learn_rates[buckets][:, None, None]
    beta_list = beta_values[buckets][:, None, None]
    mom_new = beta_list * old_state + update
    step_once = (-rate_list * (update + beta_list * mom_new)).astype(jnp.bfloat16)
    weight_steps = jnp.broadcast_to(step_once[None], (DEVICES, MATS, DKV, D))
    new_momentum = jnp.zeros((DEVICES * SLOTS, DKV, D), jnp.bfloat16).at[flat_index].set(mom_new.astype(jnp.bfloat16))
    return (new_errors, weight_steps, new_momentum)
```

```python
import functools

import jax
import jax.numpy as jnp
from jax import lax
from jax.experimental import pallas as pl
from jax.experimental.pallas import tpu as pltpu
from jax.sharding import PartitionSpec as P

AXES = ("dp", "group")
F32 = jnp.float32
BF16 = jnp.bfloat16
SMEM = pl.BlockSpec(memory_space=pltpu.SMEM)


def whole(shape):
    return pl.BlockSpec(shape, lambda i: (0,) * len(shape))


def per_matrix(shape):
    return pl.BlockSpec((1,) + shape, lambda i: (i,) + (0,) * len(shape))


def split(value):
    high = value.astype(BF16)
    return high, (value - high.astype(F32)).astype(BF16)


def dot(left, right, dims):
    return lax.dot_general(left, right, (dims, ((), ())), preferred_element_type=F32)


def params():
    return pltpu.CompilerParams(dimension_semantics=("arbitrary",), vmem_limit_bytes=40 * 1024 * 1024)


def left_kernel(grad_ref, error_ref, q_ref, mine_ref, other_ref, left_ref):
    i = pl.program_id(0)
    mats = left_ref.shape[0]
    me = lax.axis_index(AXES)
    rank = q_ref.shape[1]
    merged = grad_ref[0] + error_ref[0].astype(F32)
    high, low = split(merged)
    q_both = jnp.concatenate(split(q_ref[0]), 0)
    both = dot(q_both, high, ((1,), (1,))) + dot(q_both, low, ((1,), (1,)))
    left_ref[i] = (both[:rank] + both[rank:]).reshape(left_ref.shape[1:])

    @pl.when(i == mats - 1)
    def _():
        bit = me & 1
        rows = grad_ref.shape[1]
        for m in range(mats):
            mine_ref[:, m * rows : (m + 1) * rows] = left_ref[m, bit]
            other_ref[:, m * rows : (m + 1) * rows] = left_ref[m, 1 - bit]


def gather_left(mine_ref, other_ref, left_ref, rows):
    bit = lax.axis_index(AXES) & 1
    for m in range(left_ref.shape[0]):
        left_ref[m, bit] = mine_ref[:, m * rows : (m + 1) * rows]
        left_ref[m, 1 - bit] = other_ref[:, m * rows : (m + 1) * rows]


def right_kernel(mine_ref, other_ref, grad_ref, error_ref, all_ref, k0_ref, k2_ref, s_ref, left_ref, right_ref):
    i = pl.program_id(0)
    low_bits = lax.axis_index(AXES) & 3
    rows = grad_ref.shape[1]

    @pl.when(i == 0)
    def _():
        gather_left(mine_ref, other_ref, left_ref, rows)

    merged = grad_ref[0] + error_ref[0].astype(F32)
    high, low = split(merged)
    left = left_ref[i].reshape(-1, rows)
    rank = left.shape[0]
    l_both = jnp.concatenate(split(left), 0)
    both = dot(l_both, high, ((1,), (0,))) + dot(l_both, low, ((1,), (0,)))
    total = both[:rank] + both[rank:]
    all_ref[0] = total
    right_ref[...] = total.reshape(right_ref.shape)
    k0_ref[0] = right_ref[low_bits]
    k2_ref[0] = right_ref[low_bits ^ 2]
    s_ref[0, 0] = right_ref[low_bits ^ 1]
    s_ref[1, 0] = right_ref[low_bits ^ 3]


def three(left):
    high, low = split(left)
    return jnp.concatenate([high, high, low], 0)


def three_right(right):
    high, low = split(right)
    return jnp.concatenate([high, low, high], 0)


def error_kernel(mine_ref, other_ref, grad_ref, error_ref, all_ref, new_ref, w_ref, left_ref):
    i = pl.program_id(0)
    rows = grad_ref.shape[1]

    @pl.when(i == 0)
    def _():
        gather_left(mine_ref, other_ref, left_ref, rows)

    left = left_ref[i].reshape(-1, rows)
    rank = left.shape[0]
    gram = lax.dot_general(
        left, left, (((1,), (1,)), ((), ())), precision=lax.Precision.HIGHEST, preferred_element_type=F32
    )
    lane = lax.broadcasted_iota(jnp.int32, (rank, rank), 1)
    line = lax.broadcasted_iota(jnp.int32, (rank, 1), 0)

    def eliminate(k, carry):
        gram, solved = carry
        column = jnp.sum(jnp.where(lane == k, gram, 0.0), 1, keepdims=True)
        is_k = line == k
        gram_row = jnp.sum(jnp.where(is_k, gram, 0.0), 0, keepdims=True)
        solved_row = jnp.sum(jnp.where(is_k, solved, 0.0), 0, keepdims=True)
        pivot = jnp.sum(jnp.where(is_k, column, 0.0), 0, keepdims=True)
        gram_row, solved_row = gram_row / pivot, solved_row / pivot
        return (
            jnp.where(is_k, gram_row, gram - column * gram_row),
            jnp.where(is_k, solved_row, solved - column * solved_row),
        )

    _, solved = lax.fori_loop(0, rank, eliminate, (gram, left))
    w = three(solved).T
    w_ref[0] = w
    approx = dot(w, three_right(all_ref[0]), ((1,), (0,)))
    new_ref[0] = (grad_ref[0] + error_ref[0].astype(F32) - approx).astype(BF16)


def slot_of(owners_ref, i):
    slot = jnp.int32(0)
    for j in range(owners_ref.shape[0]):
        slot += jnp.where((j < i) & (owners_ref[j] == owners_ref[i]), 1, 0).astype(jnp.int32)
    return slot


OLD_ORDER = ((0,), (4,), (2, 6), (1, 5, 3, 7))


def old_kernel(owners_ref, mom_ref, k0_ref, k4_ref, k26_ref, odd_ref):
    me = lax.axis_index(AXES)
    outs = (k0_ref, k4_ref, k26_ref, odd_ref)
    for i in range(owners_ref.shape[0]):
        own = owners_ref[i] == me
        slot = slot_of(owners_ref, i)

        @pl.when(own)
        def _():
            for out, order in zip(outs, OLD_ORDER):
                for n, position in enumerate(order):
                    out[n, i] = mom_ref[slot, position ^ (me & 7)]

        @pl.when(jnp.logical_not(own))
        def _():
            for out, order in zip(outs, OLD_ORDER):
                for n in range(len(order)):
                    out[n, i] = jnp.zeros(out.shape[2:], BF16)


def step_kernel(
    owners_ref, buckets_ref, rates_ref, betas_ref,
    r0_ref, r1_ref, r2_ref, r3_ref, w_ref, o0_ref, o4_ref, o2_ref, o6_ref, o1_ref, o5_ref, o3_ref, o7_ref,
    step_ref, mom_ref, right_ref, update_ref,
):
    i = pl.program_id(0)
    me = lax.axis_index(AXES)
    rate = rates_ref[buckets_ref[i]]
    beta = betas_ref[buckets_ref[i]]

    @pl.when(i == 0)
    def _():
        mom_ref[...] = jnp.zeros_like(mom_ref)

    for position, ref in enumerate((r0_ref, r1_ref, r2_ref, r3_ref)):
        right_ref[position ^ (me & 3)] = ref[0]
    right = three_right(right_ref[...].reshape(-1, right_ref.shape[2]))
    update_ref[...] = dot(w_ref[0], right, ((1,), (0,))).reshape(update_ref.shape)
    own = owners_ref[i] == me
    slot = slot_of(owners_ref, i)
    olds = (o0_ref, o1_ref, o2_ref, o3_ref, o4_ref, o5_ref, o6_ref, o7_ref)
    for position, ref in enumerate(olds):
        piece = position ^ (me & 7)
        update = update_ref[piece]
        mom = beta * ref[0, 0].astype(F32) + update
        step_ref[0, piece] = (-rate * (update + beta * mom)).astype(BF16)

        @pl.when(own)
        def _():
            mom_ref[slot, piece] = mom.astype(BF16)


def exchange(value, mask, count):
    return lax.ppermute(value, AXES, [(d, d ^ mask) for d in range(count)])


def total_over(value, bits, count):
    while bits:
        head, bits = bits[:2], bits[2:]
        masks = [1 << head[0]] if len(head) == 1 else [1 << head[0], 1 << head[1], (1 << head[0]) | (1 << head[1])]
        value = functools.reduce(jnp.add, [exchange(value, m, count) for m in masks], value)
    return value


def on_device(count, gradients, errors, q_init, owners, buckets, learn_rates, beta_values, momentum):
    grads, errs = gradients[0], errors[0]
    mats, rows, cols = grads.shape
    rank = q_init.shape[2]
    slots = momentum.shape[0]
    bits = list(range(count.bit_length() - 1))
    q_t = jnp.swapaxes(q_init, 1, 2)
    half, quarter, piece = rank // 2, rank // 4, rows // 8
    grad_spec = per_matrix((rows, cols))
    sds = jax.ShapeDtypeStruct

    mine, other = pl.pallas_call(
        left_kernel,
        grid=(mats,),
        in_specs=[grad_spec, grad_spec, per_matrix((rank, cols))],
        out_specs=[whole((half, mats * rows))] * 2,
        out_shape=[sds((half, mats * rows), F32)] * 2,
        scratch_shapes=[pltpu.VMEM((mats, 2, half, rows), F32)],
        compiler_params=params(),
        name="left",
    )(grads, errs, q_t)

    def old_shape(n):
        return (n, mats, piece, cols)

    sizes = [len(order) for order in OLD_ORDER]
    k0, k4, k26, odd = pl.pallas_call(
        old_kernel,
        grid=(1,),
        in_specs=[SMEM, whole((slots, 8, piece, cols))],
        out_specs=[whole(old_shape(n)) for n in sizes],
        out_shape=[sds(old_shape(n), BF16) for n in sizes],
        compiler_params=params(),
        name="old",
    )(owners, momentum.reshape(slots, 8, piece, cols))

    got = exchange(odd, 1, count)
    got2 = exchange(k26 + got[2:], 2, count)
    k0, k4 = k0 + got[0:1] + got2[0:1], k4 + got[1:2] + got2[1:2]
    v0 = k0 + exchange(k4, 4, count)
    for bit in bits[3:]:
        v0 = v0 + exchange(v0, 1 << bit, count)
    v4 = exchange(v0, 4, count)
    v2 = exchange(v0, 2, count)
    v6 = exchange(v4, 2, count)
    v1, v5, v3, v7 = (exchange(v, 1, count) for v in (v0, v4, v2, v6))

    mine = mine + exchange(other, 1, count)
    mine = total_over(mine, bits[1:], count)
    other = exchange(mine, 1, count)

    right_all, keep, send2, send = pl.pallas_call(
        right_kernel,
        grid=(mats,),
        in_specs=[whole((half, mats * rows))] * 2 + [grad_spec, grad_spec],
        out_specs=[
            per_matrix((rank, cols)),
            per_matrix((quarter, cols)),
            per_matrix((quarter, cols)),
            pl.BlockSpec((2, 1, quarter, cols), lambda i: (0, i, 0, 0)),
        ],
        out_shape=[
            sds((mats, rank, cols), F32),
            sds((mats, quarter, cols), F32),
            sds((mats, quarter, cols), F32),
            sds((2, mats, quarter, cols), F32),
        ],
        scratch_shapes=[pltpu.VMEM((mats, 2, half, rows), F32), pltpu.VMEM((4, quarter, cols), F32)],
        compiler_params=params(),
        name="right",
    )(mine, other, grads, errs)

    new_errors, w = pl.pallas_call(
        error_kernel,
        grid=(mats,),
        in_specs=[whole((half, mats * rows))] * 2 + [grad_spec, grad_spec, per_matrix((rank, cols))],
        out_specs=[grad_spec, per_matrix((rows, 3 * rank))],
        out_shape=[sds((mats, rows, cols), BF16), sds((mats, rows, 3 * rank), BF16)],
        scratch_shapes=[pltpu.VMEM((mats, 2, half, rows), F32)],
        compiler_params=params(),
        name="errors",
    )(mine, other, grads, errs, right_all)

    got = exchange(send, 1, count)
    r0 = keep + got[0] + exchange(send2 + got[1], 2, count)
    r0 = total_over(total_over(r0, bits[2:3], count), bits[3:], count)
    r2 = exchange(r0, 2, count)
    r1 = exchange(r0, 1, count)
    r3 = exchange(r2, 1, count)

    quarter_spec = per_matrix((quarter, cols))
    old_spec = pl.BlockSpec((1, 1, piece, cols), lambda i: (0, i, 0, 0))
    steps, new_mom = pl.pallas_call(
        step_kernel,
        grid=(mats,),
        in_specs=[SMEM] * 4 + [quarter_spec] * 4 + [per_matrix((rows, 3 * rank))] + [old_spec] * 8,
        out_specs=[per_matrix((8, piece, cols)), whole((slots, 8, piece, cols))],
        out_shape=[sds((mats, 8, piece, cols), BF16), sds((slots, 8, piece, cols), BF16)],
        scratch_shapes=[pltpu.VMEM((4, quarter, cols), F32), pltpu.VMEM((8, piece, cols), F32)],
        compiler_params=params(),
        name="step",
    )(owners, buckets, learn_rates, beta_values, r0, r1, r2, r3, w, v0, v4, v2, v6, v1, v5, v3, v7)
    return (new_errors[None], steps.reshape(1, mats, rows, cols), new_mom.reshape(momentum.shape))


def solution(mesh):
    count = mesh.shape["dp"] * mesh.shape["group"]
    rep = P(AXES, None, None, None)
    return jax.shard_map(
        functools.partial(on_device, count),
        mesh=mesh,
        in_specs=(rep, rep, P(), P(), P(), P(), P(), P(AXES, None, None)),
        out_specs=(rep, rep, P(AXES, None, None)),
        check_vma=False,
    )
```

```python
import functools

import jax
import jax.numpy as jnp
from jax import lax
from jax.experimental import pallas as pl
from jax.experimental.pallas import tpu as pltpu
from jax.sharding import PartitionSpec as P

AXES = ("dp", "group")
F32 = jnp.float32
BF16 = jnp.bfloat16
SMEM = pl.BlockSpec(memory_space=pltpu.SMEM)


def whole(shape):
    return pl.BlockSpec(shape, lambda i: (0,) * len(shape))


def per_matrix(shape):
    return pl.BlockSpec((1,) + shape, lambda i: (i,) + (0,) * len(shape))


def split(value):
    high = value.astype(BF16)
    return high, (value - high.astype(F32)).astype(BF16)


def dot(left, right, dims):
    return lax.dot_general(left, right, (dims, ((), ())), preferred_element_type=F32)


def params():
    return pltpu.CompilerParams(dimension_semantics=("arbitrary",), vmem_limit_bytes=40 * 1024 * 1024)


def cost(mebibytes):
    return pl.CostEstimate(flops=0, transcendentals=0, bytes_accessed=mebibytes * 1024 * 1024)


def after(value, *others):
    return lax.optimization_barrier((value,) + others)[0]


def left_kernel(grad_ref, error_ref, q_ref, mine_ref, other_ref, left_ref):
    i = pl.program_id(0)
    mats = left_ref.shape[0]
    me = lax.axis_index(AXES)
    rank = q_ref.shape[1]
    merged = grad_ref[0] + error_ref[0].astype(F32)
    high, low = split(merged)
    q_both = jnp.concatenate(split(q_ref[0]), 0)
    both = dot(q_both, high, ((1,), (1,))) + dot(q_both, low, ((1,), (1,)))
    left_ref[i] = (both[:rank] + both[rank:]).reshape(left_ref.shape[1:])

    @pl.when(i == mats - 1)
    def _():
        bit = me & 1
        rows = grad_ref.shape[1]
        for m in range(mats):
            mine_ref[:, m * rows : (m + 1) * rows] = left_ref[m, bit]
            other_ref[:, m * rows : (m + 1) * rows] = left_ref[m, 1 - bit]


def gather_left(mine_ref, other_ref, left_ref, rows):
    bit = lax.axis_index(AXES) & 1
    for m in range(left_ref.shape[0]):
        left_ref[m, bit] = mine_ref[:, m * rows : (m + 1) * rows]
        left_ref[m, 1 - bit] = other_ref[:, m * rows : (m + 1) * rows]


def right_kernel(mine_ref, other_ref, grad_ref, error_ref, all_ref, k0_ref, k2_ref, s_ref, left_ref, right_ref):
    i = pl.program_id(0)
    low_bits = lax.axis_index(AXES) & 3
    rows = grad_ref.shape[1]

    @pl.when(i == 0)
    def _():
        gather_left(mine_ref, other_ref, left_ref, rows)

    merged = grad_ref[0] + error_ref[0].astype(F32)
    high, low = split(merged)
    left = left_ref[i].reshape(-1, rows)
    rank = left.shape[0]
    l_both = jnp.concatenate(split(left), 0)
    both = dot(l_both, high, ((1,), (0,))) + dot(l_both, low, ((1,), (0,)))
    total = both[:rank] + both[rank:]
    all_ref[0] = total
    right_ref[...] = total.reshape(right_ref.shape)
    k0_ref[0] = right_ref[low_bits]
    k2_ref[0] = right_ref[low_bits ^ 2]
    s_ref[0, 0] = right_ref[low_bits ^ 1]
    s_ref[1, 0] = right_ref[low_bits ^ 3]


def three(left):
    high, low = split(left)
    return jnp.concatenate([high, high, low], 0)


def three_right(right):
    high, low = split(right)
    return jnp.concatenate([high, low, high], 0)


def solve_kernel(mine_ref, other_ref, w_ref, left_ref):
    mats, _, half, rows = left_ref.shape
    rank = 2 * half
    gather_left(mine_ref, other_ref, left_ref, rows)
    left = left_ref[...].reshape(mats, rank, rows)

    def exact(x, y, contract):
        return jnp.stack(
            [
                lax.dot_general(
                    x[m], y[m], (contract, ((), ())), precision=lax.Precision.HIGHEST, preferred_element_type=F32
                )
                for m in range(mats)
            ]
        )

    gram = exact(left, left, ((1,), (1,)))
    line = lax.broadcasted_iota(jnp.int32, gram.shape, 1)
    lane = lax.broadcasted_iota(jnp.int32, gram.shape, 2)
    for k in range(rank):
        inverse = 1.0 / gram[:, k : k + 1, k : k + 1]
        row = jnp.where(lane[:, k : k + 1] == k, inverse, gram[:, k : k + 1] * inverse)
        rest = jnp.where(lane == k, 0.0, gram) - gram[:, :, k : k + 1] * row
        gram = jnp.where(line == k, row, rest)
    solved = exact(gram, left, ((1,), (0,)))
    for m in range(mats):
        w_ref[m] = three(solved[m]).T


def error_kernel(grad_ref, error_ref, w_ref, all_ref, new_ref):
    approx = dot(w_ref[0], three_right(all_ref[0]), ((1,), (0,)))
    new_ref[0] = (grad_ref[0] + error_ref[0].astype(F32) - approx).astype(BF16)


def slot_of(owners_ref, i):
    slot = jnp.int32(0)
    for j in range(owners_ref.shape[0]):
        slot += jnp.where((j < i) & (owners_ref[j] == owners_ref[i]), 1, 0).astype(jnp.int32)
    return slot


OLD_ORDER = ((0,), (2,), (4,), (6,), (1, 3, 5, 7))


def old_kernel(owners_ref, mom_ref, k0_ref, k2_ref, k4_ref, k6_ref, odd_ref):
    me = lax.axis_index(AXES)
    outs = (k0_ref, k2_ref, k4_ref, k6_ref, odd_ref)
    for i in range(owners_ref.shape[0]):
        own = owners_ref[i] == me
        slot = slot_of(owners_ref, i)

        @pl.when(own)
        def _():
            for out, order in zip(outs, OLD_ORDER):
                for n, position in enumerate(order):
                    out[n, i] = mom_ref[slot, position ^ (me & 7)]

        @pl.when(jnp.logical_not(own))
        def _():
            for out, order in zip(outs, OLD_ORDER):
                for n in range(len(order)):
                    out[n, i] = jnp.zeros(out.shape[2:], BF16)


def step_kernel(
    owners_ref, buckets_ref, rates_ref, betas_ref,
    r0_ref, r1_ref, r2_ref, r3_ref, w_ref, o0_ref, o1_ref, o2_ref, o3_ref, o4_ref, o5_ref, o6_ref, o7_ref,
    step_ref, mom_ref, right_ref, update_ref,
):
    i = pl.program_id(0)
    me = lax.axis_index(AXES)
    rate = rates_ref[buckets_ref[i]]
    beta = betas_ref[buckets_ref[i]]

    @pl.when(i == 0)
    def _():
        mom_ref[...] = jnp.zeros_like(mom_ref)

    for position, ref in enumerate((r0_ref, r1_ref, r2_ref, r3_ref)):
        right_ref[position ^ (me & 3)] = ref[0]
    right = three_right(right_ref[...].reshape(-1, right_ref.shape[2]))
    update_ref[...] = dot(w_ref[0], right, ((1,), (0,))).reshape(update_ref.shape)
    own = owners_ref[i] == me
    slot = slot_of(owners_ref, i)
    olds = (o0_ref, o1_ref, o2_ref, o3_ref, o4_ref, o5_ref, o6_ref, o7_ref)
    for position, ref in enumerate(olds):
        piece = position ^ (me & 7)
        update = update_ref[piece]
        mom = beta * ref[0, 0].astype(F32) + update
        step_ref[0, piece] = (-rate * (update + beta * mom)).astype(BF16)

        @pl.when(own)
        def _():
            mom_ref[slot, piece] = mom.astype(BF16)


def exchange(value, mask, count):
    return lax.ppermute(value, AXES, [(d, d ^ mask) for d in range(count)])


def total_over(value, bits, count):
    while bits:
        head, bits = bits[:2], bits[2:]
        masks = [1 << head[0]] if len(head) == 1 else [1 << head[0], 1 << head[1], (1 << head[0]) | (1 << head[1])]
        value = functools.reduce(jnp.add, [exchange(value, m, count) for m in masks], value)
    return value


def on_device(count, gradients, errors, q_init, owners, buckets, learn_rates, beta_values, momentum):
    grads, errs = gradients[0], errors[0]
    mats, rows, cols = grads.shape
    rank = q_init.shape[2]
    slots = momentum.shape[0]
    bits = list(range(count.bit_length() - 1))
    q_t = jnp.swapaxes(q_init, 1, 2)
    half, quarter, piece = rank // 2, rank // 4, rows // 8
    grad_spec = per_matrix((rows, cols))
    sds = jax.ShapeDtypeStruct

    mine, other = pl.pallas_call(
        left_kernel,
        grid=(mats,),
        in_specs=[grad_spec, grad_spec, per_matrix((rank, cols))],
        out_specs=[whole((half, mats * rows))] * 2,
        out_shape=[sds((half, mats * rows), F32)] * 2,
        scratch_shapes=[pltpu.VMEM((mats, 2, half, rows), F32)],
        compiler_params=params(),
        name="left",
    )(grads, errs, q_t)

    def old_shape(n):
        return (n, mats, piece, cols)

    sizes = [len(order) for order in OLD_ORDER]
    *evens, odd = pl.pallas_call(
        old_kernel,
        grid=(1,),
        in_specs=[SMEM, whole((slots, 8, piece, cols))],
        out_specs=[whole(old_shape(n)) for n in sizes],
        out_shape=[sds(old_shape(n), BF16) for n in sizes],
        compiler_params=params(),
        name="old",
    )(owners, after(momentum.reshape(slots, 8, piece, cols), mine))

    def swap(value, mask):
        return exchange(value, mask, count)

    got = swap(odd, 1)
    mine = mine + swap(other, 1)
    evens = [after(even + got[n : n + 1], mine) for n, even in enumerate(evens)]
    mine = total_over(mine, bits[1:3], count)
    old = evens[0] + swap(evens[1], 2) + swap(evens[2], 4) + swap(evens[3], 6)
    old = after(old, mine)
    mine = total_over(mine, bits[3:], count)
    other = swap(mine, 1)

    right_all, keep, send2, send = pl.pallas_call(
        right_kernel,
        grid=(mats,),
        in_specs=[whole((half, mats * rows))] * 2 + [grad_spec, grad_spec],
        out_specs=[
            per_matrix((rank, cols)),
            per_matrix((quarter, cols)),
            per_matrix((quarter, cols)),
            pl.BlockSpec((2, 1, quarter, cols), lambda i: (0, i, 0, 0)),
        ],
        out_shape=[
            sds((mats, rank, cols), F32),
            sds((mats, quarter, cols), F32),
            sds((mats, quarter, cols), F32),
            sds((2, mats, quarter, cols), F32),
        ],
        scratch_shapes=[pltpu.VMEM((mats, 2, half, rows), F32), pltpu.VMEM((4, quarter, cols), F32)],
        compiler_params=params(),
        name="right",
    )(mine, other, grads, errs)

    w = pl.pallas_call(
        solve_kernel,
        grid=(1,),
        in_specs=[whole((half, mats * rows))] * 2,
        out_specs=whole((mats, rows, 3 * rank)),
        out_shape=sds((mats, rows, 3 * rank), BF16),
        scratch_shapes=[pltpu.VMEM((mats, 2, half, rows), F32)],
        compiler_params=params(),
        cost_estimate=cost(16),
        name="solve",
    )(mine, other)

    for bit in bits[3:-1]:
        old = old + swap(old, 1 << bit)
    got = swap(send, 1)
    send2 = send2 + got[1]
    old = after(old, send2)
    r0 = keep + got[0] + swap(send2, 2)
    old = old + swap(old, 1 << bits[-1])
    r0 = total_over(r0, bits[2:3], count)
    w = after(w, r0)
    new_errors = pl.pallas_call(
        error_kernel,
        grid=(mats,),
        in_specs=[grad_spec, grad_spec, per_matrix((rows, 3 * rank)), per_matrix((rank, cols))],
        out_specs=grad_spec,
        out_shape=sds((mats, rows, cols), BF16),
        compiler_params=params(),
        cost_estimate=cost(12),
        name="errors",
    )(grads, errs, w, right_all)
    olds = {0: after(old, r0)}
    for mask in (2, 4, 6):
        olds[mask] = swap(olds[0], mask)
    r0 = total_over(r0, bits[3:], count)
    r0 = after(r0, new_errors)
    r1, r2, r3 = (swap(r0, mask) for mask in (1, 2, 3))
    for mask in (0, 2, 4, 6):
        olds[mask + 1] = swap(olds[mask], 1)

    quarter_spec = per_matrix((quarter, cols))
    old_spec = pl.BlockSpec((1, 1, piece, cols), lambda i: (0, i, 0, 0))
    steps, new_mom = pl.pallas_call(
        step_kernel,
        grid=(mats,),
        in_specs=[SMEM] * 4 + [quarter_spec] * 4 + [per_matrix((rows, 3 * rank))] + [old_spec] * 8,
        out_specs=[per_matrix((8, piece, cols)), whole((slots, 8, piece, cols))],
        out_shape=[sds((mats, 8, piece, cols), BF16), sds((slots, 8, piece, cols), BF16)],
        scratch_shapes=[pltpu.VMEM((4, quarter, cols), F32), pltpu.VMEM((8, piece, cols), F32)],
        compiler_params=params(),
        name="step",
    )(owners, buckets, learn_rates, beta_values, r0, r1, r2, r3, w, *(olds[n] for n in range(8)))
    return (new_errors[None], steps.reshape(1, mats, rows, cols), new_mom.reshape(momentum.shape))


def solution(mesh):
    count = mesh.shape["dp"] * mesh.shape["group"]
    rep = P(AXES, None, None, None)
    return jax.shard_map(
        functools.partial(on_device, count),
        mesh=mesh,
        in_specs=(rep, rep, P(), P(), P(), P(), P(), P(AXES, None, None)),
        out_specs=(rep, rep, P(AXES, None, None)),
        check_vma=False,
    )
```

```python
import functools

import jax
import jax.numpy as jnp
from jax import lax
from jax.experimental import pallas as pl
from jax.experimental.pallas import tpu as pltpu
from jax.sharding import PartitionSpec as P

AXES = ("dp", "group")
F32 = jnp.float32
BF16 = jnp.bfloat16
SMEM = pl.BlockSpec(memory_space=pltpu.SMEM)


def whole(shape):
    return pl.BlockSpec(shape, lambda i: (0,) * len(shape))


def per_matrix(shape):
    return pl.BlockSpec((1,) + shape, lambda i: (i,) + (0,) * len(shape))


def split(value):
    high = value.astype(BF16)
    return high, (value - high.astype(F32)).astype(BF16)


def dot(left, right, dims):
    return lax.dot_general(left, right, (dims, ((), ())), preferred_element_type=F32)


def params(mebibytes=40):
    return pltpu.CompilerParams(dimension_semantics=("arbitrary",), vmem_limit_bytes=mebibytes * 1024 * 1024)


def cost(mebibytes):
    return pl.CostEstimate(flops=0, transcendentals=0, bytes_accessed=mebibytes * 1024 * 1024)


def after(value, *others):
    return lax.optimization_barrier((value,) + others)[0]


def left_kernel(grad_ref, error_ref, q_ref, mine_ref, other_ref, left_ref):
    i = pl.program_id(0)
    mats = left_ref.shape[0]
    me = lax.axis_index(AXES)
    rank = q_ref.shape[1]
    merged = grad_ref[0] + error_ref[0].astype(F32)
    high, low = split(merged)
    q_both = jnp.concatenate(split(q_ref[0]), 0)
    both = dot(q_both, high, ((1,), (1,))) + dot(q_both, low, ((1,), (1,)))
    left_ref[i] = (both[:rank] + both[rank:]).reshape(left_ref.shape[1:])

    @pl.when(i == mats - 1)
    def _():
        bit = me & 1
        rows = grad_ref.shape[1]
        for m in range(mats):
            mine_ref[:, m * rows : (m + 1) * rows] = left_ref[m, bit]
            other_ref[:, m * rows : (m + 1) * rows] = left_ref[m, 1 - bit]


def gather_left(mine_ref, other_ref, left_ref, rows):
    bit = lax.axis_index(AXES) & 1
    for m in range(left_ref.shape[0]):
        left_ref[m, bit] = mine_ref[:, m * rows : (m + 1) * rows]
        left_ref[m, 1 - bit] = other_ref[:, m * rows : (m + 1) * rows]


def right_kernel(mine_ref, other_ref, grad_ref, error_ref, all_ref, k0_ref, k2_ref, s_ref, left_ref, right_ref):
    i = pl.program_id(0)
    low_bits = lax.axis_index(AXES) & 3
    rows = grad_ref.shape[1]

    @pl.when(i == 0)
    def _():
        gather_left(mine_ref, other_ref, left_ref, rows)

    merged = grad_ref[0] + error_ref[0].astype(F32)
    high, low = split(merged)
    left = left_ref[i].reshape(-1, rows)
    rank = left.shape[0]
    l_both = jnp.concatenate(split(left), 0)
    both = dot(l_both, high, ((1,), (0,))) + dot(l_both, low, ((1,), (0,)))
    total = both[:rank] + both[rank:]
    all_ref[0] = total
    right_ref[...] = total.reshape(right_ref.shape)
    k0_ref[0] = right_ref[low_bits]
    k2_ref[0] = right_ref[low_bits ^ 2]
    s_ref[0, 0] = right_ref[low_bits ^ 1]
    s_ref[1, 0] = right_ref[low_bits ^ 3]


def three(left):
    high, low = split(left)
    return jnp.concatenate([high, high, low], 0)


def three_right(right):
    high, low = split(right)
    return jnp.concatenate([high, low, high], 0)


def solve_kernel(mine_ref, other_ref, w_ref, left_ref):
    mats, _, half, rows = left_ref.shape
    rank = 2 * half
    gather_left(mine_ref, other_ref, left_ref, rows)
    left = left_ref[...].reshape(mats, rank, rows)

    def exact(x, y, contract):
        return jnp.stack(
            [
                lax.dot_general(
                    x[m], y[m], (contract, ((), ())), precision=lax.Precision.HIGHEST, preferred_element_type=F32
                )
                for m in range(mats)
            ]
        )

    gram = exact(left, left, ((1,), (1,)))
    line = lax.broadcasted_iota(jnp.int32, gram.shape, 1)
    lane = lax.broadcasted_iota(jnp.int32, gram.shape, 2)
    for k in range(rank):
        inverse = 1.0 / gram[:, k : k + 1, k : k + 1]
        row = jnp.where(lane[:, k : k + 1] == k, inverse, gram[:, k : k + 1] * inverse)
        rest = jnp.where(lane == k, 0.0, gram) - gram[:, :, k : k + 1] * row
        gram = jnp.where(line == k, row, rest)
    solved = exact(gram, left, ((1,), (0,)))
    for m in range(mats):
        w_ref[m] = three(solved[m]).T


def error_kernel(grad_ref, error_ref, w_ref, all_ref, new_ref):
    approx = dot(w_ref[0], three_right(all_ref[0]), ((1,), (0,)))
    new_ref[0] = (grad_ref[0] + error_ref[0].astype(F32) - approx).astype(BF16)


def slot_of(owners_ref, i):
    slot = jnp.int32(0)
    for j in range(owners_ref.shape[0]):
        slot += jnp.where((j < i) & (owners_ref[j] == owners_ref[i]), 1, 0).astype(jnp.int32)
    return slot


OLD_ORDER = ((0,), (2,), (4,), (6,), (1, 3, 5, 7))


def old_kernel(owners_ref, mom_ref, k0_ref, k2_ref, k4_ref, k6_ref, odd_ref):
    me = lax.axis_index(AXES)
    outs = (k0_ref, k2_ref, k4_ref, k6_ref, odd_ref)
    for i in range(owners_ref.shape[0]):
        own = owners_ref[i] == me
        slot = slot_of(owners_ref, i)

        @pl.when(own)
        def _():
            for out, order in zip(outs, OLD_ORDER):
                for n, position in enumerate(order):
                    out[n, i] = mom_ref[slot, position ^ (me & 7)]

        @pl.when(jnp.logical_not(own))
        def _():
            for out, order in zip(outs, OLD_ORDER):
                for n in range(len(order)):
                    out[n, i] = jnp.zeros(out.shape[2:], BF16)


def step_kernel(
    owners_ref, buckets_ref, rates_ref, betas_ref,
    r0_ref, r1_ref, r2_ref, r3_ref, w_ref, even_ref, odd_ref,
    step_ref, mom_ref, right_ref, update_ref,
):
    i = pl.program_id(0)
    me = lax.axis_index(AXES)
    rate = rates_ref[buckets_ref[i]]
    beta = betas_ref[buckets_ref[i]]

    @pl.when(i == 0)
    def _():
        mom_ref[...] = jnp.zeros_like(mom_ref)

    for position, ref in enumerate((r0_ref, r1_ref, r2_ref, r3_ref)):
        right_ref[position ^ (me & 3)] = ref[0]
    right = three_right(right_ref[...].reshape(-1, right_ref.shape[2]))
    update_ref[...] = dot(w_ref[0], right, ((1,), (0,))).reshape(update_ref.shape)
    own = owners_ref[i] == me
    slot = slot_of(owners_ref, i)
    for position in range(8):
        ref = (even_ref, odd_ref)[position % 2]
        piece = position ^ (me & 7)
        update = update_ref[piece]
        mom = beta * ref[position // 2, 0].astype(F32) + update
        step_ref[0, piece] = (-rate * (update + beta * mom)).astype(BF16)

        @pl.when(own)
        def _():
            mom_ref[slot, piece] = mom.astype(BF16)


def exchange(value, mask, count):
    return lax.ppermute(value, AXES, [(d, d ^ mask) for d in range(count)])


def total_over(value, bits, count):
    while bits:
        head, bits = bits[:2], bits[2:]
        masks = [1 << head[0]] if len(head) == 1 else [1 << head[0], 1 << head[1], (1 << head[0]) | (1 << head[1])]
        value = functools.reduce(jnp.add, [exchange(value, m, count) for m in masks], value)
    return value


def on_device(count, gradients, errors, q_init, owners, buckets, learn_rates, beta_values, momentum):
    grads, errs = gradients[0], errors[0]
    mats, rows, cols = grads.shape
    rank = q_init.shape[2]
    slots = momentum.shape[0]
    bits = list(range(count.bit_length() - 1))
    q_t = jnp.swapaxes(q_init, 1, 2)
    half, quarter, piece = rank // 2, rank // 4, rows // 8
    grad_spec = per_matrix((rows, cols))
    sds = jax.ShapeDtypeStruct

    mine, other = pl.pallas_call(
        left_kernel,
        grid=(mats,),
        in_specs=[grad_spec, grad_spec, per_matrix((rank, cols))],
        out_specs=[whole((half, mats * rows))] * 2,
        out_shape=[sds((half, mats * rows), F32)] * 2,
        scratch_shapes=[pltpu.VMEM((mats, 2, half, rows), F32)],
        compiler_params=params(61),
        name="left",
    )(grads, errs, q_t)

    def old_shape(n):
        return (n, mats, piece, cols)

    def swap(value, mask):
        return exchange(value, mask, count)

    mine = mine + swap(other, 1)
    sizes = [len(order) for order in OLD_ORDER]
    *evens, odd = pl.pallas_call(
        old_kernel,
        grid=(1,),
        in_specs=[SMEM, whole((slots, 8, piece, cols))],
        out_specs=[whole(old_shape(n)) for n in sizes],
        out_shape=[sds(old_shape(n), BF16) for n in sizes],
        compiler_params=params(),
        name="old",
    )(owners, after(momentum.reshape(slots, 8, piece, cols), mine))

    got = swap(odd, 1)
    evens = [even + got[n : n + 1] for n, even in enumerate(evens)]
    mine = total_over(mine, bits[1:3], count)
    mine = after(mine, *evens)
    got = [swap(evens[n], 2 * n) for n in (1, 2, 3)]
    mine = total_over(mine, bits[3:], count)
    old = after(evens[0], mine) + got[0] + got[1] + got[2]
    other = swap(after(mine, old), 1)

    right_all, keep, send2, send = pl.pallas_call(
        right_kernel,
        grid=(mats,),
        in_specs=[whole((half, mats * rows))] * 2 + [grad_spec, grad_spec],
        out_specs=[
            per_matrix((rank, cols)),
            per_matrix((quarter, cols)),
            per_matrix((quarter, cols)),
            pl.BlockSpec((2, 1, quarter, cols), lambda i: (0, i, 0, 0)),
        ],
        out_shape=[
            sds((mats, rank, cols), F32),
            sds((mats, quarter, cols), F32),
            sds((mats, quarter, cols), F32),
            sds((2, mats, quarter, cols), F32),
        ],
        scratch_shapes=[pltpu.VMEM((mats, 2, half, rows), F32), pltpu.VMEM((4, quarter, cols), F32)],
        compiler_params=params(),
        name="right",
    )(mine, other, grads, errs)

    w = pl.pallas_call(
        solve_kernel,
        grid=(1,),
        in_specs=[whole((half, mats * rows))] * 2,
        out_specs=whole((mats, rows, 3 * rank)),
        out_shape=sds((mats, rows, 3 * rank), BF16),
        scratch_shapes=[pltpu.VMEM((mats, 2, half, rows), F32)],
        compiler_params=params(),
        cost_estimate=cost(16),
        name="solve",
    )(mine, other)

    got = swap(send, 1)
    send2 = send2 + got[1]
    for bit in bits[3:-1]:
        from_other = swap(old, 1 << bit)
        old = after(old, send2) + from_other
    send2 = after(send2, old)
    from_other = swap(old, 1 << bits[-1])
    r0 = keep + got[0] + swap(send2, 2)
    r0 = total_over(r0, bits[2:3], count)
    old = after(old, r0) + from_other
    r0 = after(r0, old)
    got = [swap(old, mask) for mask in (2, 4, 6)]
    r0 = after(total_over(r0, bits[3:], count), w)
    r1, r2, r3 = (swap(r0, mask) for mask in (1, 2, 3))
    old = after(old, r0)
    evens = jnp.concatenate([old] + got)
    odds = swap(evens, 1)
    new_errors = pl.pallas_call(
        error_kernel,
        grid=(mats,),
        in_specs=[grad_spec, grad_spec, per_matrix((rows, 3 * rank)), per_matrix((rank, cols))],
        out_specs=grad_spec,
        out_shape=sds((mats, rows, cols), BF16),
        compiler_params=params(),
        cost_estimate=cost(12),
        name="errors",
    )(grads, errs, after(w, evens), right_all)
    w = after(w, new_errors)

    quarter_spec = per_matrix((quarter, cols))
    old_spec = pl.BlockSpec((4, 1, piece, cols), lambda i: (0, i, 0, 0))
    steps, new_mom = pl.pallas_call(
        step_kernel,
        grid=(mats,),
        in_specs=[SMEM] * 4 + [quarter_spec] * 4 + [per_matrix((rows, 3 * rank))] + [old_spec] * 2,
        out_specs=[per_matrix((8, piece, cols)), whole((slots, 8, piece, cols))],
        out_shape=[sds((mats, 8, piece, cols), BF16), sds((slots, 8, piece, cols), BF16)],
        scratch_shapes=[pltpu.VMEM((4, quarter, cols), F32), pltpu.VMEM((8, piece, cols), F32)],
        compiler_params=params(),
        name="step",
    )(owners, buckets, learn_rates, beta_values, r0, r1, r2, r3, w, evens, odds)
    return (new_errors[None], steps.reshape(1, mats, rows, cols), new_mom.reshape(momentum.shape))


def solution(mesh):
    count = mesh.shape["dp"] * mesh.shape["group"]
    rep = P(AXES, None, None, None)
    return jax.shard_map(
        functools.partial(on_device, count),
        mesh=mesh,
        in_specs=(rep, rep, P(), P(), P(), P(), P(), P(AXES, None, None)),
        out_specs=(rep, rep, P(AXES, None, None)),
        check_vma=False,
    )
```

```python
import functools

import jax
import jax.numpy as jnp
from jax import lax
from jax.experimental import pallas as pl
from jax.experimental.pallas import tpu as pltpu
from jax.sharding import PartitionSpec as P

AXES = ("dp", "group")
F32 = jnp.float32
BF16 = jnp.bfloat16
SMEM = pl.BlockSpec(memory_space=pltpu.SMEM)


def whole(shape):
    return pl.BlockSpec(shape, lambda i: (0,) * len(shape))


def per_matrix(shape):
    return pl.BlockSpec((1,) + shape, lambda i: (i,) + (0,) * len(shape))


def split(value):
    high = value.astype(BF16)
    return high, (value - high.astype(F32)).astype(BF16)


def dot(left, right, dims):
    return lax.dot_general(left, right, (dims, ((), ())), preferred_element_type=F32)


def params(mebibytes=40):
    return pltpu.CompilerParams(dimension_semantics=("arbitrary",), vmem_limit_bytes=mebibytes * 1024 * 1024)


def cost(mebibytes):
    return pl.CostEstimate(flops=0, transcendentals=0, bytes_accessed=mebibytes * 1024 * 1024)


def after(value, *others):
    return lax.optimization_barrier((value,) + others)[0]


def left_kernel(grad_hbm, error_hbm, q_hbm, mine_ref, other_ref, grad_ref, error_ref, q_ref, left_ref, sems):
    mats, rows, _ = grad_ref.shape
    rank = q_ref.shape[1]
    pairs = ((grad_hbm, grad_ref), (error_hbm, error_ref), (q_hbm, q_ref))
    copies = [
        [pltpu.make_async_copy(hbm.at[m], ref.at[m], sems.at[m, n]) for n, (hbm, ref) in enumerate(pairs)]
        for m in range(mats)
    ]
    for per_mat in copies:
        for copy in per_mat:
            copy.start()
    bit = lax.axis_index(AXES) & 1
    for m in range(mats):
        for copy in copies[m]:
            copy.wait()
        high, low = split(grad_ref[m] + error_ref[m].astype(F32))
        q_both = jnp.concatenate(split(q_ref[m]), 0)
        both = dot(q_both, high, ((1,), (1,))) + dot(q_both, low, ((1,), (1,)))
        left_ref[...] = (both[:rank] + both[rank:]).reshape(left_ref.shape)
        mine_ref[:, m * rows : (m + 1) * rows] = left_ref[bit]
        other_ref[:, m * rows : (m + 1) * rows] = left_ref[1 - bit]


def gather_left(mine_ref, other_ref, left_ref, rows):
    bit = lax.axis_index(AXES) & 1
    for m in range(left_ref.shape[0]):
        left_ref[m, bit] = mine_ref[:, m * rows : (m + 1) * rows]
        left_ref[m, 1 - bit] = other_ref[:, m * rows : (m + 1) * rows]


def right_kernel(mine_ref, other_ref, grad_ref, error_ref, all_ref, k0_ref, k2_ref, s_ref, left_ref, right_ref):
    i = pl.program_id(0)
    low_bits = lax.axis_index(AXES) & 3
    rows = grad_ref.shape[1]

    @pl.when(i == 0)
    def _():
        gather_left(mine_ref, other_ref, left_ref, rows)

    merged = grad_ref[0] + error_ref[0].astype(F32)
    high, low = split(merged)
    left = left_ref[i].reshape(-1, rows)
    rank = left.shape[0]
    l_both = jnp.concatenate(split(left), 0)
    both = dot(l_both, high, ((1,), (0,))) + dot(l_both, low, ((1,), (0,)))
    total = both[:rank] + both[rank:]
    all_ref[0] = total
    right_ref[...] = total.reshape(right_ref.shape)
    k0_ref[0] = right_ref[low_bits]
    k2_ref[0] = right_ref[low_bits ^ 2]
    s_ref[0, 0] = right_ref[low_bits ^ 1]
    s_ref[1, 0] = right_ref[low_bits ^ 3]


def three(left):
    high, low = split(left)
    return jnp.concatenate([high, high, low], 0)


def three_right(right):
    high, low = split(right)
    return jnp.concatenate([high, low, high], 0)


def solve_kernel(mine_ref, other_ref, w_ref, left_ref):
    mats, _, half, rows = left_ref.shape
    rank = 2 * half
    gather_left(mine_ref, other_ref, left_ref, rows)
    left = left_ref[...].reshape(mats, rank, rows)

    def exact(x, y, contract):
        return jnp.stack(
            [
                lax.dot_general(
                    x[m], y[m], (contract, ((), ())), precision=lax.Precision.HIGHEST, preferred_element_type=F32
                )
                for m in range(mats)
            ]
        )

    gram = exact(left, left, ((1,), (1,)))
    line = lax.broadcasted_iota(jnp.int32, gram.shape, 1)
    lane = lax.broadcasted_iota(jnp.int32, gram.shape, 2)
    for k in range(rank):
        inverse = 1.0 / gram[:, k : k + 1, k : k + 1]
        row = jnp.where(lane[:, k : k + 1] == k, inverse, gram[:, k : k + 1] * inverse)
        rest = jnp.where(lane == k, 0.0, gram) - gram[:, :, k : k + 1] * row
        gram = jnp.where(line == k, row, rest)
    solved = exact(gram, left, ((1,), (0,)))
    for m in range(mats):
        w_ref[m] = three(solved[m]).T


def error_kernel(grad_ref, error_ref, w_ref, all_ref, new_ref):
    approx = dot(w_ref[0], three_right(all_ref[0]), ((1,), (0,)))
    new_ref[0] = (grad_ref[0] + error_ref[0].astype(F32) - approx).astype(BF16)


def slot_of(owners_ref, i):
    slot = jnp.int32(0)
    for j in range(owners_ref.shape[0]):
        slot += jnp.where((j < i) & (owners_ref[j] == owners_ref[i]), 1, 0).astype(jnp.int32)
    return slot


OLD_ORDER = ((0,), (2,), (4,), (6,), (1, 3, 5, 7))


def old_kernel(owners_ref, mom_ref, k0_ref, k2_ref, k4_ref, k6_ref, odd_ref):
    me = lax.axis_index(AXES)
    outs = (k0_ref, k2_ref, k4_ref, k6_ref, odd_ref)
    for i in range(owners_ref.shape[0]):
        own = owners_ref[i] == me
        slot = slot_of(owners_ref, i)

        @pl.when(own)
        def _():
            for out, order in zip(outs, OLD_ORDER):
                for n, position in enumerate(order):
                    out[n, i] = mom_ref[slot, position ^ (me & 7)]

        @pl.when(jnp.logical_not(own))
        def _():
            for out, order in zip(outs, OLD_ORDER):
                for n in range(len(order)):
                    out[n, i] = jnp.zeros(out.shape[2:], BF16)


def step_kernel(
    owners_ref, buckets_ref, rates_ref, betas_ref,
    r0_ref, r1_ref, r2_ref, r3_ref, w_ref, even_ref, odd_ref,
    step_ref, mom_ref, right_ref, update_ref,
):
    i = pl.program_id(0)
    me = lax.axis_index(AXES)
    rate = rates_ref[buckets_ref[i]]
    beta = betas_ref[buckets_ref[i]]

    @pl.when(i == 0)
    def _():
        mom_ref[...] = jnp.zeros_like(mom_ref)

    for position, ref in enumerate((r0_ref, r1_ref, r2_ref, r3_ref)):
        right_ref[position ^ (me & 3)] = ref[0]
    right = three_right(right_ref[...].reshape(-1, right_ref.shape[2]))
    update_ref[...] = dot(w_ref[0], right, ((1,), (0,))).reshape(update_ref.shape)
    own = owners_ref[i] == me
    slot = slot_of(owners_ref, i)
    for position in range(8):
        ref = (even_ref, odd_ref)[position % 2]
        piece = position ^ (me & 7)
        update = update_ref[piece]
        mom = beta * ref[position // 2, 0].astype(F32) + update
        step_ref[0, piece] = (-rate * (update + beta * mom)).astype(BF16)

        @pl.when(own)
        def _():
            mom_ref[slot, piece] = mom.astype(BF16)


def exchange(value, mask, count):
    return lax.ppermute(value, AXES, [(d, d ^ mask) for d in range(count)])


def total_over(value, bits, count):
    while bits:
        head, bits = bits[:2], bits[2:]
        masks = [1 << head[0]] if len(head) == 1 else [1 << head[0], 1 << head[1], (1 << head[0]) | (1 << head[1])]
        value = functools.reduce(jnp.add, [exchange(value, m, count) for m in masks], value)
    return value


def on_device(count, gradients, errors, q_init, owners, buckets, learn_rates, beta_values, momentum):
    grads, errs = gradients[0], errors[0]
    mats, rows, cols = grads.shape
    rank = q_init.shape[2]
    slots = momentum.shape[0]
    bits = list(range(count.bit_length() - 1))
    q_t = jnp.swapaxes(q_init, 1, 2)
    half, quarter, piece = rank // 2, rank // 4, rows // 8
    grad_spec = per_matrix((rows, cols))
    sds = jax.ShapeDtypeStruct

    def old_shape(n):
        return (n, mats, piece, cols)

    def swap(value, mask):
        return exchange(value, mask, count)

    sizes = [len(order) for order in OLD_ORDER]
    *evens, odd = pl.pallas_call(
        old_kernel,
        grid=(1,),
        in_specs=[SMEM, whole((slots, 8, piece, cols))],
        out_specs=[whole(old_shape(n)) for n in sizes],
        out_shape=[sds(old_shape(n), BF16) for n in sizes],
        compiler_params=params(),
        name="old",
    )(owners, momentum.reshape(slots, 8, piece, cols))

    mine, other = pl.pallas_call(
        left_kernel,
        in_specs=[pl.BlockSpec(memory_space=pltpu.HBM)] * 3,
        out_shape=[sds((half, mats * rows), F32)] * 2,
        scratch_shapes=[
            pltpu.VMEM((mats, rows, cols), F32),
            pltpu.VMEM((mats, rows, cols), BF16),
            pltpu.VMEM((mats, rank, cols), F32),
            pltpu.VMEM((2, half, rows), F32),
            pltpu.SemaphoreType.DMA((mats, 3)),
        ],
        compiler_params=pltpu.CompilerParams(vmem_limit_bytes=60 * 1024 * 1024),
        name="left",
    )(grads, errs, after(q_t, odd))

    got = swap(odd, 1)
    evens = [after(evens[n], mine) + got[n : n + 1] for n in range(4)]
    mine = mine + swap(after(other, *evens), 1)
    got = [swap(evens[n], 2 * n) for n in (1, 2, 3)]
    for bit in bits[1:3]:
        mine = total_over(mine, [bit], count)
    old = after(evens[0], mine) + got[0] + got[1] + got[2]
    mine = after(mine, old)
    from_other = swap(old, 1 << bits[3])
    mine = total_over(mine, bits[3:], count)
    old = after(old, mine) + from_other
    other = swap(after(mine, old), 1)

    right_all, keep, send2, send = pl.pallas_call(
        right_kernel,
        grid=(mats,),
        in_specs=[whole((half, mats * rows))] * 2 + [grad_spec, grad_spec],
        out_specs=[
            per_matrix((rank, cols)),
            per_matrix((quarter, cols)),
            per_matrix((quarter, cols)),
            pl.BlockSpec((2, 1, quarter, cols), lambda i: (0, i, 0, 0)),
        ],
        out_shape=[
            sds((mats, rank, cols), F32),
            sds((mats, quarter, cols), F32),
            sds((mats, quarter, cols), F32),
            sds((2, mats, quarter, cols), F32),
        ],
        scratch_shapes=[pltpu.VMEM((mats, 2, half, rows), F32), pltpu.VMEM((4, quarter, cols), F32)],
        compiler_params=params(),
        name="right",
    )(mine, other, grads, errs)

    w = pl.pallas_call(
        solve_kernel,
        grid=(1,),
        in_specs=[whole((half, mats * rows))] * 2,
        out_specs=whole((mats, rows, 3 * rank)),
        out_shape=sds((mats, rows, 3 * rank), BF16),
        scratch_shapes=[pltpu.VMEM((mats, 2, half, rows), F32)],
        compiler_params=params(),
        cost_estimate=cost(16),
        name="solve",
    )(mine, other)

    got = swap(send, 1)
    r0 = keep + got[0] + swap(send2 + got[1], 2)
    for bit in bits[4:-1]:
        old = old + swap(old, 1 << bit)
    from_other = swap(old, 1 << bits[-1])
    r0 = total_over(r0, bits[2:3], count)
    old = after(old, r0) + from_other
    r0 = after(r0, old)
    got = [swap(old, mask) for mask in (2, 4, 6)]
    for bit in bits[3:-1]:
        r0 = total_over(r0, [bit], count)
    r0 = total_over(after(r0, w), bits[-1:], count)
    evens = jnp.concatenate([after(old, r0)] + got)
    r0 = after(r0, evens)
    odds = swap(evens, 1)
    r1, r2, r3 = (swap(r0, mask) for mask in (1, 2, 3))
    new_errors = pl.pallas_call(
        error_kernel,
        grid=(mats,),
        in_specs=[grad_spec, grad_spec, per_matrix((rows, 3 * rank)), per_matrix((rank, cols))],
        out_specs=grad_spec,
        out_shape=sds((mats, rows, cols), BF16),
        compiler_params=params(),
        cost_estimate=cost(12),
        name="errors",
    )(grads, errs, after(w, evens), right_all)
    w = after(w, new_errors)

    quarter_spec = per_matrix((quarter, cols))
    old_spec = pl.BlockSpec((4, 1, piece, cols), lambda i: (0, i, 0, 0))
    steps, new_mom = pl.pallas_call(
        step_kernel,
        grid=(mats,),
        in_specs=[SMEM] * 4 + [quarter_spec] * 4 + [per_matrix((rows, 3 * rank))] + [old_spec] * 2,
        out_specs=[per_matrix((8, piece, cols)), whole((slots, 8, piece, cols))],
        out_shape=[sds((mats, 8, piece, cols), BF16), sds((slots, 8, piece, cols), BF16)],
        scratch_shapes=[pltpu.VMEM((4, quarter, cols), F32), pltpu.VMEM((8, piece, cols), F32)],
        compiler_params=params(),
        name="step",
    )(owners, buckets, learn_rates, beta_values, r0, r1, r2, r3, w, evens, odds)
    return (new_errors[None], steps.reshape(1, mats, rows, cols), new_mom.reshape(momentum.shape))


def solution(mesh):
    count = mesh.shape["dp"] * mesh.shape["group"]
    rep = P(AXES, None, None, None)
    return jax.shard_map(
        functools.partial(on_device, count),
        mesh=mesh,
        in_specs=(rep, rep, P(), P(), P(), P(), P(), P(AXES, None, None)),
        out_specs=(rep, rep, P(AXES, None, None)),
        check_vma=False,
    )
```

```python
import functools

import jax
import jax.numpy as jnp
from jax import lax
from jax.experimental import pallas as pl
from jax.experimental.pallas import tpu as pltpu
from jax.sharding import PartitionSpec as P

AXES = ("dp", "group")
F32 = jnp.float32
BF16 = jnp.bfloat16
SMEM = pl.BlockSpec(memory_space=pltpu.SMEM)


def whole(shape):
    return pl.BlockSpec(shape, lambda i: (0,) * len(shape))


def per_matrix(shape):
    return pl.BlockSpec((1,) + shape, lambda i: (i,) + (0,) * len(shape))


def split(value):
    high = value.astype(BF16)
    return high, (value - high.astype(F32)).astype(BF16)


def dot(left, right, dims):
    return lax.dot_general(left, right, (dims, ((), ())), preferred_element_type=F32)


def params(mebibytes=40):
    return pltpu.CompilerParams(dimension_semantics=("arbitrary",), vmem_limit_bytes=mebibytes * 1024 * 1024)


def cost(mebibytes):
    return pl.CostEstimate(flops=0, transcendentals=0, bytes_accessed=mebibytes * 1024 * 1024)


def after(value, *others):
    return lax.optimization_barrier((value,) + others)[0]


def left_kernel(grad_hbm, error_hbm, q_hbm, mine_ref, other_ref, grad_ref, error_ref, q_ref, left_ref, sems):
    mats, rows, _ = grad_ref.shape
    rank = q_ref.shape[1]
    pairs = ((grad_hbm, grad_ref), (error_hbm, error_ref), (q_hbm, q_ref))
    copies = [
        [pltpu.make_async_copy(hbm.at[m], ref.at[m], sems.at[m, n]) for n, (hbm, ref) in enumerate(pairs)]
        for m in range(mats)
    ]
    for per_mat in copies:
        for copy in per_mat:
            copy.start()
    bit = lax.axis_index(AXES) & 1
    for m in range(mats):
        for copy in copies[m]:
            copy.wait()
        high, low = split(grad_ref[m] + error_ref[m].astype(F32))
        q_both = jnp.concatenate(split(q_ref[m]), 0)
        both = dot(q_both, high, ((1,), (1,))) + dot(q_both, low, ((1,), (1,)))
        left_ref[...] = (both[:rank] + both[rank:]).reshape(left_ref.shape)
        mine_ref[:, m * rows : (m + 1) * rows] = left_ref[bit]
        other_ref[:, m * rows : (m + 1) * rows] = left_ref[1 - bit]


def gather_left(mine_ref, other_ref, left_ref, rows):
    bit = lax.axis_index(AXES) & 1
    for m in range(left_ref.shape[0]):
        left_ref[m, bit] = mine_ref[:, m * rows : (m + 1) * rows]
        left_ref[m, 1 - bit] = other_ref[:, m * rows : (m + 1) * rows]


def right_kernel(mine_ref, other_ref, grad_ref, error_ref, all_ref, k0_ref, k2_ref, s_ref, left_ref, right_ref):
    i = pl.program_id(0)
    low_bits = lax.axis_index(AXES) & 3
    rows = grad_ref.shape[1]

    @pl.when(i == 0)
    def _():
        gather_left(mine_ref, other_ref, left_ref, rows)

    merged = grad_ref[0] + error_ref[0].astype(F32)
    high, low = split(merged)
    left = left_ref[i].reshape(-1, rows)
    rank = left.shape[0]
    l_both = jnp.concatenate(split(left), 0)
    both = dot(l_both, high, ((1,), (0,))) + dot(l_both, low, ((1,), (0,)))
    total = both[:rank] + both[rank:]
    all_ref[0] = total
    right_ref[...] = total.reshape(right_ref.shape)
    k0_ref[0] = right_ref[low_bits]
    k2_ref[0] = right_ref[low_bits ^ 2]
    s_ref[0, 0] = right_ref[low_bits ^ 1]
    s_ref[1, 0] = right_ref[low_bits ^ 3]


def three(left):
    high, low = split(left)
    return jnp.concatenate([high, high, low], 0)


def three_right(right):
    high, low = split(right)
    return jnp.concatenate([high, low, high], 0)


def solve_kernel(mine_ref, other_ref, w_ref, left_ref):
    mats, _, half, rows = left_ref.shape
    rank = 2 * half
    gather_left(mine_ref, other_ref, left_ref, rows)
    left = left_ref[...].reshape(mats, rank, rows)

    def exact(x, y, contract):
        return jnp.stack(
            [
                lax.dot_general(
                    x[m], y[m], (contract, ((), ())), precision=lax.Precision.HIGHEST, preferred_element_type=F32
                )
                for m in range(mats)
            ]
        )

    gram = exact(left, left, ((1,), (1,)))
    line = lax.broadcasted_iota(jnp.int32, gram.shape, 1)
    lane = lax.broadcasted_iota(jnp.int32, gram.shape, 2)
    for k in range(rank):
        inverse = 1.0 / gram[:, k : k + 1, k : k + 1]
        row = jnp.where(lane[:, k : k + 1] == k, inverse, gram[:, k : k + 1] * inverse)
        rest = jnp.where(lane == k, 0.0, gram) - gram[:, :, k : k + 1] * row
        gram = jnp.where(line == k, row, rest)
    solved = exact(gram, left, ((1,), (0,)))
    for m in range(mats):
        w_ref[m] = three(solved[m]).T


def error_kernel(grad_ref, error_ref, w_ref, all_ref, new_ref):
    approx = dot(w_ref[0], three_right(all_ref[0]), ((1,), (0,)))
    new_ref[0] = (grad_ref[0] + error_ref[0].astype(F32) - approx).astype(BF16)


def slot_of(owners_ref, i):
    slot = jnp.int32(0)
    for j in range(owners_ref.shape[0]):
        slot += jnp.where((j < i) & (owners_ref[j] == owners_ref[i]), 1, 0).astype(jnp.int32)
    return slot


OLD_ORDER = ((0,), (2,), (4,), (6,), (1, 3, 5, 7))


def old_kernel(owners_ref, mom_ref, k0_ref, k2_ref, k4_ref, k6_ref, odd_ref):
    me = lax.axis_index(AXES)
    outs = (k0_ref, k2_ref, k4_ref, k6_ref, odd_ref)
    for i in range(owners_ref.shape[0]):
        own = owners_ref[i] == me
        slot = slot_of(owners_ref, i)

        @pl.when(own)
        def _():
            for out, order in zip(outs, OLD_ORDER):
                for n, position in enumerate(order):
                    out[n, i] = mom_ref[slot, position ^ (me & 7)]

        @pl.when(jnp.logical_not(own))
        def _():
            for out, order in zip(outs, OLD_ORDER):
                for n in range(len(order)):
                    out[n, i] = jnp.zeros(out.shape[2:], BF16)


def step_kernel(
    owners_ref, buckets_ref, rates_ref, betas_ref,
    r0_ref, r1_ref, r2_ref, r3_ref, w_ref, even_ref, odd_ref,
    step_ref, mom_ref, right_ref, update_ref,
):
    i = pl.program_id(0)
    me = lax.axis_index(AXES)
    rate = rates_ref[buckets_ref[i]]
    beta = betas_ref[buckets_ref[i]]

    @pl.when(i == 0)
    def _():
        mom_ref[...] = jnp.zeros_like(mom_ref)

    for position, ref in enumerate((r0_ref, r1_ref, r2_ref, r3_ref)):
        right_ref[position ^ (me & 3)] = ref[0]
    right = three_right(right_ref[...].reshape(-1, right_ref.shape[2]))
    update_ref[...] = dot(w_ref[0], right, ((1,), (0,))).reshape(update_ref.shape)
    own = owners_ref[i] == me
    slot = slot_of(owners_ref, i)
    for position in range(8):
        ref = (even_ref, odd_ref)[position % 2]
        piece = position ^ (me & 7)
        update = update_ref[piece]
        mom = beta * ref[position // 2, 0].astype(F32) + update
        step_ref[0, piece] = (-rate * (update + beta * mom)).astype(BF16)

        @pl.when(own)
        def _():
            mom_ref[slot, piece] = mom.astype(BF16)


def exchange(value, mask, count):
    return lax.ppermute(value, AXES, [(d, d ^ mask) for d in range(count)])


def total_over(value, bits, count):
    while bits:
        head, bits = bits[:2], bits[2:]
        masks = [1 << head[0]] if len(head) == 1 else [1 << head[0], 1 << head[1], (1 << head[0]) | (1 << head[1])]
        value = functools.reduce(jnp.add, [exchange(value, m, count) for m in masks], value)
    return value


def on_device(count, gradients, errors, q_init, owners, buckets, learn_rates, beta_values, momentum):
    grads, errs = gradients[0], errors[0]
    mats, rows, cols = grads.shape
    rank = q_init.shape[2]
    slots = momentum.shape[0]
    bits = list(range(count.bit_length() - 1))
    q_t = jnp.swapaxes(q_init, 1, 2)
    half, quarter, piece = rank // 2, rank // 4, rows // 8
    grad_spec = per_matrix((rows, cols))
    sds = jax.ShapeDtypeStruct

    def old_shape(n):
        return (n, mats, piece, cols)

    def swap(value, mask):
        return exchange(value, mask, count)

    sizes = [len(order) for order in OLD_ORDER]
    *evens, odd = pl.pallas_call(
        old_kernel,
        grid=(1,),
        in_specs=[SMEM, whole((slots, 8, piece, cols))],
        out_specs=[whole(old_shape(n)) for n in sizes],
        out_shape=[sds(old_shape(n), BF16) for n in sizes],
        compiler_params=params(),
        name="old",
    )(owners, momentum.reshape(slots, 8, piece, cols))

    mine, other = pl.pallas_call(
        left_kernel,
        in_specs=[pl.BlockSpec(memory_space=pltpu.HBM)] * 3,
        out_shape=[sds((half, mats * rows), F32)] * 2,
        scratch_shapes=[
            pltpu.VMEM((mats, rows, cols), F32),
            pltpu.VMEM((mats, rows, cols), BF16),
            pltpu.VMEM((mats, rank, cols), F32),
            pltpu.VMEM((2, half, rows), F32),
            pltpu.SemaphoreType.DMA((mats, 3)),
        ],
        compiler_params=pltpu.CompilerParams(vmem_limit_bytes=60 * 1024 * 1024),
        name="left",
    )(grads, errs, after(q_t, odd))

    got = swap(odd, 1)
    evens = [after(evens[n], mine) + got[n : n + 1] for n in range(4)]
    mine = mine + swap(after(other, *evens), 1)
    got = [swap(evens[n], 2 * n) for n in (1, 2, 3)]
    for bit in bits[3:]:
        mine = total_over(mine, [bit], count)
    old = after(evens[0], mine) + got[0] + got[1] + got[2]
    mine = after(mine, old)
    from_other = swap(old, 1 << bits[3])
    mine = total_over(mine, bits[1:3], count)
    old = after(old, mine) + from_other
    other = swap(mine, 1)

    right_all, keep, send2, send = pl.pallas_call(
        right_kernel,
        grid=(mats,),
        in_specs=[whole((half, mats * rows))] * 2 + [grad_spec, grad_spec],
        out_specs=[
            per_matrix((rank, cols)),
            per_matrix((quarter, cols)),
            per_matrix((quarter, cols)),
            pl.BlockSpec((2, 1, quarter, cols), lambda i: (0, i, 0, 0)),
        ],
        out_shape=[
            sds((mats, rank, cols), F32),
            sds((mats, quarter, cols), F32),
            sds((mats, quarter, cols), F32),
            sds((2, mats, quarter, cols), F32),
        ],
        scratch_shapes=[pltpu.VMEM((mats, 2, half, rows), F32), pltpu.VMEM((4, quarter, cols), F32)],
        compiler_params=params(),
        name="right",
    )(mine, other, grads, errs)

    w = pl.pallas_call(
        solve_kernel,
        grid=(1,),
        in_specs=[whole((half, mats * rows))] * 2,
        out_specs=whole((mats, rows, 3 * rank)),
        out_shape=sds((mats, rows, 3 * rank), BF16),
        scratch_shapes=[pltpu.VMEM((mats, 2, half, rows), F32)],
        compiler_params=params(),
        cost_estimate=cost(16),
        name="solve",
    )(mine, other)

    got = swap(after(send, old), 1)
    r0 = keep + got[0] + swap(send2 + got[1], 2)
    for bit in bits[4:-1]:
        old = old + swap(old, 1 << bit)
    from_other = swap(old, 1 << bits[-1])
    r0 = total_over(r0, bits[2:3], count)
    old = after(old, r0) + from_other
    r0 = after(r0, old, w)
    got = [swap(old, mask) for mask in (2, 4, 6)]
    for bit in bits[3:]:
        r0 = total_over(r0, [bit], count)
    evens = jnp.concatenate([after(old, r0)] + got)
    r0 = after(r0, evens)
    odds = swap(evens, 1)
    r1, r2, r3 = (swap(r0, mask) for mask in (1, 2, 3))
    new_errors = pl.pallas_call(
        error_kernel,
        grid=(mats,),
        in_specs=[grad_spec, grad_spec, per_matrix((rows, 3 * rank)), per_matrix((rank, cols))],
        out_specs=grad_spec,
        out_shape=sds((mats, rows, cols), BF16),
        compiler_params=params(),
        cost_estimate=cost(12),
        name="errors",
    )(grads, errs, after(w, evens), right_all)
    w = after(w, new_errors)

    quarter_spec = per_matrix((quarter, cols))
    old_spec = pl.BlockSpec((4, 1, piece, cols), lambda i: (0, i, 0, 0))
    steps, new_mom = pl.pallas_call(
        step_kernel,
        grid=(mats,),
        in_specs=[SMEM] * 4 + [quarter_spec] * 4 + [per_matrix((rows, 3 * rank))] + [old_spec] * 2,
        out_specs=[per_matrix((8, piece, cols)), whole((slots, 8, piece, cols))],
        out_shape=[sds((mats, 8, piece, cols), BF16), sds((slots, 8, piece, cols), BF16)],
        scratch_shapes=[pltpu.VMEM((4, quarter, cols), F32), pltpu.VMEM((8, piece, cols), F32)],
        compiler_params=params(),
        name="step",
    )(owners, buckets, learn_rates, beta_values, r0, r1, r2, r3, w, evens, odds)
    return (new_errors[None], steps.reshape(1, mats, rows, cols), new_mom.reshape(momentum.shape))


def solution(mesh):
    count = mesh.shape["dp"] * mesh.shape["group"]
    rep = P(AXES, None, None, None)
    return jax.shard_map(
        functools.partial(on_device, count),
        mesh=mesh,
        in_specs=(rep, rep, P(), P(), P(), P(), P(), P(AXES, None, None)),
        out_specs=(rep, rep, P(AXES, None, None)),
        check_vma=False,
    )
```

```python
import functools

import jax
import jax.numpy as jnp
from jax import lax
from jax.experimental import pallas as pl
from jax.experimental.pallas import tpu as pltpu
from jax.sharding import PartitionSpec as P

AXES = ("dp", "group")
F32 = jnp.float32
BF16 = jnp.bfloat16
SMEM = pl.BlockSpec(memory_space=pltpu.SMEM)
LIMIT = 53


def whole(shape):
    return pl.BlockSpec(shape, lambda i: (0,) * len(shape))


def per_matrix(shape):
    return pl.BlockSpec((1,) + shape, lambda i: (i,) + (0,) * len(shape))


def split(value):
    high = value.astype(BF16)
    return high, (value - high.astype(F32)).astype(BF16)


def dot(left, right, dims):
    return lax.dot_general(left, right, (dims, ((), ())), preferred_element_type=F32)


def params(mebibytes=40):
    return pltpu.CompilerParams(dimension_semantics=("arbitrary",), vmem_limit_bytes=mebibytes * 1024 * 1024)


def cost(mebibytes):
    return pl.CostEstimate(flops=0, transcendentals=0, bytes_accessed=mebibytes * 1024 * 1024)


def after(value, *others):
    return lax.optimization_barrier((value,) + others)[0]


def gather_left(mine_ref, other_ref, left_ref, rows):
    bit = lax.axis_index(AXES) & 1
    for m in range(left_ref.shape[0]):
        left_ref[m, bit] = mine_ref[:, m * rows : (m + 1) * rows]
        left_ref[m, 1 - bit] = other_ref[:, m * rows : (m + 1) * rows]


def right_kernel(mine_ref, other_ref, grad_ref, error_ref, all_ref, k0_ref, k2_ref, s_ref, left_ref, right_ref):
    i = pl.program_id(0)
    low_bits = lax.axis_index(AXES) & 3
    rows = grad_ref.shape[1]

    @pl.when(i == 0)
    def _():
        gather_left(mine_ref, other_ref, left_ref, rows)

    merged = grad_ref[0] + error_ref[0].astype(F32)
    high, low = split(merged)
    left = left_ref[i].reshape(-1, rows)
    rank = left.shape[0]
    l_both = jnp.concatenate(split(left), 0)
    both = dot(l_both, high, ((1,), (0,))) + dot(l_both, low, ((1,), (0,)))
    total = both[:rank] + both[rank:]
    all_ref[0] = total
    right_ref[...] = total.reshape(right_ref.shape)
    k0_ref[0] = right_ref[low_bits]
    k2_ref[0] = right_ref[low_bits ^ 2]
    s_ref[0, 0] = right_ref[low_bits ^ 1]
    s_ref[1, 0] = right_ref[low_bits ^ 3]


def three(left):
    high, low = split(left)
    return jnp.concatenate([high, high, low], 0)


def three_right(right):
    high, low = split(right)
    return jnp.concatenate([high, low, high], 0)


def solve_kernel(mine_ref, other_ref, w_ref, left_ref):
    mats, _, half, rows = left_ref.shape
    rank = 2 * half
    gather_left(mine_ref, other_ref, left_ref, rows)
    left = left_ref[...].reshape(mats, rank, rows)

    def exact(x, y, contract):
        return jnp.stack(
            [
                lax.dot_general(
                    x[m], y[m], (contract, ((), ())), precision=lax.Precision.HIGHEST, preferred_element_type=F32
                )
                for m in range(mats)
            ]
        )

    gram = exact(left, left, ((1,), (1,)))
    line = lax.broadcasted_iota(jnp.int32, gram.shape, 1)
    lane = lax.broadcasted_iota(jnp.int32, gram.shape, 2)
    for k in range(rank):
        inverse = 1.0 / gram[:, k : k + 1, k : k + 1]
        row = jnp.where(lane[:, k : k + 1] == k, inverse, gram[:, k : k + 1] * inverse)
        rest = jnp.where(lane == k, 0.0, gram) - gram[:, :, k : k + 1] * row
        gram = jnp.where(line == k, row, rest)
    solved = exact(gram, left, ((1,), (0,)))
    for m in range(mats):
        w_ref[m] = three(solved[m]).T


def error_kernel(grad_ref, error_ref, w_ref, all_ref, new_ref):
    approx = dot(w_ref[0], three_right(all_ref[0]), ((1,), (0,)))
    new_ref[0] = (grad_ref[0] + error_ref[0].astype(F32) - approx).astype(BF16)


def slot_of(owners_ref, i):
    slot = jnp.int32(0)
    for j in range(owners_ref.shape[0]):
        slot += jnp.where((j < i) & (owners_ref[j] == owners_ref[i]), 1, 0).astype(jnp.int32)
    return slot


OLD_ORDER = ((0,), (2,), (4,), (6,), (1, 3, 5, 7))


def first_kernel(
    owners_ref, grad_hbm, error_hbm, q_hbm, mom_hbm,
    mine_ref, other_ref, k0_ref, k2_ref, k4_ref, k6_ref, odd_ref,
    grad_ref, error_ref, q_ref, mom_ref, left_ref, sems, mom_sem,
):
    mats, rows, _ = grad_ref.shape
    rank = q_ref.shape[1]
    me = lax.axis_index(AXES)
    pairs = ((grad_hbm, grad_ref), (error_hbm, error_ref), (q_hbm, q_ref))
    copies = [
        [pltpu.make_async_copy(hbm.at[m], ref.at[m], sems.at[m, n]) for n, (hbm, ref) in enumerate(pairs)]
        for m in range(mats)
    ]
    mom_copy = pltpu.make_async_copy(mom_hbm, mom_ref, mom_sem)
    for copy in copies[0]:
        copy.start()
    mom_copy.start()

    outs = (k0_ref, k2_ref, k4_ref, k6_ref, odd_ref)
    for out in outs:
        out[...] = jnp.zeros(out.shape, BF16)
    for m in range(mats):
        if m + 1 < mats:
            for copy in copies[m + 1]:
                copy.start()
        for copy in copies[m]:
            copy.wait()
        high, low = split(grad_ref[m] + error_ref[m].astype(F32))
        q_both = jnp.concatenate(split(q_ref[m]), 0)
        both = dot(q_both, high, ((1,), (1,))) + dot(q_both, low, ((1,), (1,)))
        left_ref[...] = (both[:rank] + both[rank:]).reshape(left_ref.shape)
        mine_ref[:, m * rows : (m + 1) * rows] = left_ref[me & 1]
        other_ref[:, m * rows : (m + 1) * rows] = left_ref[1 - (me & 1)]
        if m == 0:
            mom_copy.wait()
            for i in range(mats):
                slot = slot_of(owners_ref, i)

                @pl.when(owners_ref[i] == me)
                def _():
                    for out, order in zip(outs, OLD_ORDER):
                        for n, position in enumerate(order):
                            out[n, i] = mom_ref[slot, position ^ (me & 7)]


def step_kernel(
    owners_ref, buckets_ref, rates_ref, betas_ref,
    r0_ref, r1_ref, r2_ref, r3_ref, w_ref, even_ref, odd_ref,
    step_ref, mom_ref, right_ref, update_ref,
):
    i = pl.program_id(0)
    me = lax.axis_index(AXES)
    rate = rates_ref[buckets_ref[i]]
    beta = betas_ref[buckets_ref[i]]
    of_update, of_old = -rate * (1.0 + beta), -rate * beta * beta

    @pl.when(i == 0)
    def _():
        mom_ref[...] = jnp.zeros_like(mom_ref)

    for position, ref in enumerate((r0_ref, r1_ref, r2_ref, r3_ref)):
        right_ref[position ^ (me & 3)] = ref[0]
    right = three_right(right_ref[...].reshape(-1, right_ref.shape[2]))
    update_ref[...] = dot(w_ref[0], right, ((1,), (0,))).reshape(update_ref.shape)
    own = owners_ref[i] == me
    slot = slot_of(owners_ref, i)
    for position in range(8):
        ref = (even_ref, odd_ref)[position % 2]
        piece = position ^ (me & 7)
        update = update_ref[piece]
        old = ref[position // 2, 0].astype(F32)
        step_ref[0, piece] = (of_update * update + of_old * old).astype(BF16)

        @pl.when(own)
        def _():
            mom_ref[slot, piece] = (beta * old + update).astype(BF16)


def exchange(value, mask, count):
    return lax.ppermute(value, AXES, [(d, d ^ mask) for d in range(count)])


def total_over(value, bits, count):
    while bits:
        head, bits = bits[:2], bits[2:]
        masks = [1 << head[0]] if len(head) == 1 else [1 << head[0], 1 << head[1], (1 << head[0]) | (1 << head[1])]
        value = functools.reduce(jnp.add, [exchange(value, m, count) for m in masks], value)
    return value


def on_device(count, gradients, errors, q_init, owners, buckets, learn_rates, beta_values, momentum):
    grads, errs = gradients[0], errors[0]
    mats, rows, cols = grads.shape
    rank = q_init.shape[2]
    slots = momentum.shape[0]
    bits = list(range(count.bit_length() - 1))
    q_t = jnp.swapaxes(q_init, 1, 2)
    half, quarter, piece = rank // 2, rank // 4, rows // 8
    grad_spec = per_matrix((rows, cols))
    sds = jax.ShapeDtypeStruct

    def old_shape(n):
        return (n, mats, piece, cols)

    def swap(value, mask):
        return exchange(value, mask, count)

    sizes = [len(order) for order in OLD_ORDER]
    mine, other, *evens, odd = pl.pallas_call(
        first_kernel,
        in_specs=[SMEM] + [pl.BlockSpec(memory_space=pltpu.HBM)] * 4,
        out_shape=[sds((half, mats * rows), F32)] * 2 + [sds(old_shape(n), BF16) for n in sizes],
        scratch_shapes=[
            pltpu.VMEM((mats, rows, cols), F32),
            pltpu.VMEM((mats, rows, cols), BF16),
            pltpu.VMEM((mats, rank, cols), F32),
            pltpu.VMEM((slots, 8, piece, cols), BF16),
            pltpu.VMEM((2, half, rows), F32),
            pltpu.SemaphoreType.DMA((mats, 3)),
            pltpu.SemaphoreType.DMA,
        ],
        compiler_params=pltpu.CompilerParams(vmem_limit_bytes=LIMIT * 1024 * 1024),
        name="first",
    )(owners, grads, errs, q_t, momentum.reshape(slots, 8, piece, cols))

    got = swap(odd, 1)
    mine = mine + swap(other, 1)
    evens = [after(even, mine) + got[n : n + 1] for n, even in enumerate(evens)]
    got = [swap(evens[n], 2 * n) for n in (1, 2, 3)]
    mine = total_over(mine, bits[3:4], count)
    mine = after(mine, *evens)
    for bit in bits[4:]:
        mine = total_over(mine, [bit], count)
    old = after(evens[0], mine) + got[0] + got[1] + got[2]
    mine = after(mine, old)
    from_other = swap(old, 1 << bits[3])
    mine = total_over(mine, bits[1:3], count)
    old = after(old, mine) + from_other
    other = swap(mine, 1)

    right_all, keep, send2, send = pl.pallas_call(
        right_kernel,
        grid=(mats,),
        in_specs=[whole((half, mats * rows))] * 2 + [grad_spec, grad_spec],
        out_specs=[
            per_matrix((rank, cols)),
            per_matrix((quarter, cols)),
            per_matrix((quarter, cols)),
            pl.BlockSpec((2, 1, quarter, cols), lambda i: (0, i, 0, 0)),
        ],
        out_shape=[
            sds((mats, rank, cols), F32),
            sds((mats, quarter, cols), F32),
            sds((mats, quarter, cols), F32),
            sds((2, mats, quarter, cols), F32),
        ],
        scratch_shapes=[pltpu.VMEM((mats, 2, half, rows), F32), pltpu.VMEM((4, quarter, cols), F32)],
        compiler_params=params(),
        name="right",
    )(mine, other, grads, errs)

    w = pl.pallas_call(
        solve_kernel,
        grid=(1,),
        in_specs=[whole((half, mats * rows))] * 2,
        out_specs=whole((mats, rows, 3 * rank)),
        out_shape=sds((mats, rows, 3 * rank), BF16),
        scratch_shapes=[pltpu.VMEM((mats, 2, half, rows), F32)],
        compiler_params=params(),
        cost_estimate=cost(16),
        name="solve",
    )(mine, other)

    got = swap(after(send, old), 1)
    for bit in bits[4:-1]:
        old = old + swap(old, 1 << bit)
    from_other = swap(old, 1 << bits[-1])
    r0 = keep + got[0] + swap(send2 + got[1], 2)
    r0 = total_over(r0, bits[2:3], count)
    old = after(old, r0) + from_other
    r0 = after(r0, old, w)
    near = [swap(old, 2), swap(old, 4)]
    for n, bit in enumerate(bits[3:]):
        r0 = total_over(r0, [bit], count)
        if n == 0:
            near = [after(value, r0) for value in near]
            r0 = after(r0, *near)
    far = swap(near[0], 4)
    evens = jnp.concatenate([after(old, r0)] + near + [far])
    r0 = after(r0, evens)
    odds = swap(evens, 1)
    r1, r2, r3 = (swap(r0, mask) for mask in (1, 2, 3))
    new_errors = pl.pallas_call(
        error_kernel,
        grid=(mats,),
        in_specs=[grad_spec, grad_spec, per_matrix((rows, 3 * rank)), per_matrix((rank, cols))],
        out_specs=grad_spec,
        out_shape=sds((mats, rows, cols), BF16),
        compiler_params=params(),
        cost_estimate=cost(12),
        name="errors",
    )(grads, errs, after(w, evens), right_all)
    w = after(w, new_errors)

    quarter_spec = per_matrix((quarter, cols))
    old_spec = pl.BlockSpec((4, 1, piece, cols), lambda i: (0, i, 0, 0))
    steps, new_mom = pl.pallas_call(
        step_kernel,
        grid=(mats,),
        in_specs=[SMEM] * 4 + [quarter_spec] * 4 + [per_matrix((rows, 3 * rank))] + [old_spec] * 2,
        out_specs=[per_matrix((8, piece, cols)), whole((slots, 8, piece, cols))],
        out_shape=[sds((mats, 8, piece, cols), BF16), sds((slots, 8, piece, cols), BF16)],
        scratch_shapes=[pltpu.VMEM((4, quarter, cols), F32), pltpu.VMEM((8, piece, cols), F32)],
        compiler_params=params(),
        name="step",
    )(owners, buckets, learn_rates, beta_values, r0, r1, r2, r3, w, evens, odds)
    return (new_errors[None], steps.reshape(1, mats, rows, cols), new_mom.reshape(momentum.shape))


def solution(mesh):
    count = mesh.shape["dp"] * mesh.shape["group"]
    rep = P(AXES, None, None, None)
    return jax.shard_map(
        functools.partial(on_device, count),
        mesh=mesh,
        in_specs=(rep, rep, P(), P(), P(), P(), P(), P(AXES, None, None)),
        out_specs=(rep, rep, P(AXES, None, None)),
        check_vma=False,
    )
```

```python
import functools

import jax
import jax.numpy as jnp
from jax import lax
from jax.experimental import pallas as pl
from jax.experimental.pallas import tpu as pltpu
from jax.sharding import PartitionSpec as P

AXES = ("dp", "group")
F32 = jnp.float32
BF16 = jnp.bfloat16
SMEM = pl.BlockSpec(memory_space=pltpu.SMEM)


def whole(shape):
    return pl.BlockSpec(shape, lambda i: (0,) * len(shape))


def per_matrix(shape):
    return pl.BlockSpec((1,) + shape, lambda i: (i,) + (0,) * len(shape))


def split(value):
    high = value.astype(BF16)
    return high, (value - high.astype(F32)).astype(BF16)


def dot(left, right, dims):
    return lax.dot_general(left, right, (dims, ((), ())), preferred_element_type=F32)


def params(mebibytes=40):
    return pltpu.CompilerParams(dimension_semantics=("arbitrary",), vmem_limit_bytes=mebibytes * 1024 * 1024)


def cost(mebibytes):
    return pl.CostEstimate(flops=0, transcendentals=0, bytes_accessed=mebibytes * 1024 * 1024)


def after(value, *others):
    return lax.optimization_barrier((value,) + others)[0]


def gather_left(mine_ref, other_ref, left_ref, rows):
    bit = lax.axis_index(AXES) & 1
    for m in range(left_ref.shape[0]):
        left_ref[m, bit] = mine_ref[:, m * rows : (m + 1) * rows]
        left_ref[m, 1 - bit] = other_ref[:, m * rows : (m + 1) * rows]


def right_kernel(mine_ref, other_ref, grad_ref, error_ref, all_ref, k0_ref, k2_ref, s_ref, left_ref, right_ref):
    i = pl.program_id(0)
    low_bits = lax.axis_index(AXES) & 3
    rows = grad_ref.shape[1]

    @pl.when(i == 0)
    def _():
        gather_left(mine_ref, other_ref, left_ref, rows)

    merged = grad_ref[0] + error_ref[0].astype(F32)
    high, low = split(merged)
    left = left_ref[i].reshape(-1, rows)
    rank = left.shape[0]
    l_both = jnp.concatenate(split(left), 0)
    both = dot(l_both, high, ((1,), (0,))) + dot(l_both, low, ((1,), (0,)))
    total = both[:rank] + both[rank:]
    all_ref[0] = total
    right_ref[...] = total.reshape(right_ref.shape)
    k0_ref[0] = right_ref[low_bits]
    k2_ref[0] = right_ref[low_bits ^ 2]
    s_ref[0, 0] = right_ref[low_bits ^ 1]
    s_ref[1, 0] = right_ref[low_bits ^ 3]


def three(left):
    high, low = split(left)
    return jnp.concatenate([high, high, low], 0)


def three_right(right):
    high, low = split(right)
    return jnp.concatenate([high, low, high], 0)


def solve_kernel(mine_ref, other_ref, w_ref, left_ref):
    mats, _, half, rows = left_ref.shape
    rank = 2 * half
    gather_left(mine_ref, other_ref, left_ref, rows)
    left = left_ref[...].reshape(mats, rank, rows)

    def exact(x, y, contract):
        return jnp.stack(
            [
                lax.dot_general(
                    x[m], y[m], (contract, ((), ())), precision=lax.Precision.HIGHEST, preferred_element_type=F32
                )
                for m in range(mats)
            ]
        )

    gram = exact(left, left, ((1,), (1,)))
    line = lax.broadcasted_iota(jnp.int32, gram.shape, 1)
    lane = lax.broadcasted_iota(jnp.int32, gram.shape, 2)
    for k in range(rank):
        inverse = 1.0 / gram[:, k : k + 1, k : k + 1]
        row = jnp.where(lane[:, k : k + 1] == k, inverse, gram[:, k : k + 1] * inverse)
        rest = jnp.where(lane == k, 0.0, gram) - gram[:, :, k : k + 1] * row
        gram = jnp.where(line == k, row, rest)
    solved = exact(gram, left, ((1,), (0,)))
    for m in range(mats):
        w_ref[m] = three(solved[m]).T


def error_kernel(grad_ref, error_ref, w_ref, all_ref, new_ref):
    approx = dot(w_ref[0], three_right(all_ref[0]), ((1,), (0,)))
    new_ref[0] = (grad_ref[0] + error_ref[0].astype(F32) - approx).astype(BF16)


def slot_of(owners_ref, i):
    slot = jnp.int32(0)
    for j in range(owners_ref.shape[0]):
        slot += jnp.where((j < i) & (owners_ref[j] == owners_ref[i]), 1, 0).astype(jnp.int32)
    return slot


def first_kernel(
    owners_hbm, grad_hbm, error_hbm, q_hbm, mom_hbm,
    mine_ref, other_ref, odd_ref,
    owners_ref, grad_ref, error_ref, q_ref, mom_ref, left_ref, sems, mom_sems,
):
    mats, rows, _ = grad_ref.shape
    rank = q_ref.shape[1]
    me = lax.axis_index(AXES)
    pairs = ((grad_hbm, grad_ref), (error_hbm, error_ref), (q_hbm, q_ref))
    copies = [
        [pltpu.make_async_copy(hbm.at[m], ref.at[m], sems.at[m, n]) for n, (hbm, ref) in enumerate(pairs)]
        for m in range(mats)
    ]
    mom_copies = [
        pltpu.make_async_copy(mom_hbm, mom_ref, mom_sems.at[0]),
        pltpu.make_async_copy(owners_hbm, owners_ref, mom_sems.at[1]),
    ]
    for copy in copies[0] + mom_copies:
        copy.start()

    odd_ref[...] = jnp.zeros(odd_ref.shape, BF16)
    for m in range(mats):
        if m + 1 < mats:
            for copy in copies[m + 1]:
                copy.start()
        for copy in copies[m]:
            copy.wait()
        high, low = split(grad_ref[m] + error_ref[m].astype(F32))
        q_both = jnp.concatenate(split(q_ref[m]), 0)
        both = dot(q_both, high, ((1,), (1,))) + dot(q_both, low, ((1,), (1,)))
        left_ref[...] = (both[:rank] + both[rank:]).reshape(left_ref.shape)
        mine_ref[:, m * rows : (m + 1) * rows] = left_ref[me & 1]
        other_ref[:, m * rows : (m + 1) * rows] = left_ref[1 - (me & 1)]
        if m == 0:
            for copy in mom_copies:
                copy.wait()
            for i in range(mats):
                slot = slot_of(owners_ref, i)

                @pl.when(owners_ref[i] == me)
                def _():
                    for n in range(4):
                        odd_ref[n, i] = mom_ref[slot, (2 * n + 1) ^ (me & 7)]


def even_kernel(owners_ref, mom_ref, got_ref, *outs):
    me = lax.axis_index(AXES)
    for n, out in enumerate(outs):
        out[0] = got_ref[n]
    for i in range(owners_ref.shape[0]):
        slot = slot_of(owners_ref, i)

        @pl.when(owners_ref[i] == me)
        def _():
            for n, out in enumerate(outs):
                out[0, i] = mom_ref[slot, (2 * n) ^ (me & 7)]


def step_kernel(
    owners_ref, buckets_ref, rates_ref, betas_ref,
    r0_ref, r1_ref, r2_ref, r3_ref, w_ref, even_ref, odd_ref,
    step_ref, mom_ref, right_ref, update_ref,
):
    i = pl.program_id(0)
    me = lax.axis_index(AXES)
    rate = rates_ref[buckets_ref[i]]
    beta = betas_ref[buckets_ref[i]]
    of_update, of_old = -rate * (1.0 + beta), -rate * beta * beta

    @pl.when(i == 0)
    def _():
        mom_ref[...] = jnp.zeros_like(mom_ref)

    for position, ref in enumerate((r0_ref, r1_ref, r2_ref, r3_ref)):
        right_ref[position ^ (me & 3)] = ref[0]
    right = three_right(right_ref[...].reshape(-1, right_ref.shape[2]))
    update_ref[...] = dot(w_ref[0], right, ((1,), (0,))).reshape(update_ref.shape)
    own = owners_ref[i] == me
    slot = slot_of(owners_ref, i)
    for position in range(8):
        ref = (even_ref, odd_ref)[position % 2]
        piece = position ^ (me & 7)
        update = update_ref[piece]
        old = ref[position // 2, 0].astype(F32)
        step_ref[0, piece] = (of_update * update + of_old * old).astype(BF16)

        @pl.when(own)
        def _():
            mom_ref[slot, piece] = (beta * old + update).astype(BF16)


def exchange(value, mask, count):
    return lax.ppermute(value, AXES, [(d, d ^ mask) for d in range(count)])


def total_over(value, bits, count):
    while bits:
        head, bits = bits[:2], bits[2:]
        masks = [1 << head[0]] if len(head) == 1 else [1 << head[0], 1 << head[1], (1 << head[0]) | (1 << head[1])]
        value = functools.reduce(jnp.add, [exchange(value, m, count) for m in masks], value)
    return value


def on_device(count, gradients, errors, q_init, owners, buckets, learn_rates, beta_values, momentum):
    grads, errs = gradients[0], errors[0]
    mats, rows, cols = grads.shape
    rank = q_init.shape[2]
    slots = momentum.shape[0]
    bits = list(range(count.bit_length() - 1))
    q_t = jnp.swapaxes(q_init, 1, 2)
    half, quarter, piece = rank // 2, rank // 4, rows // 8
    grad_spec = per_matrix((rows, cols))
    sds = jax.ShapeDtypeStruct

    def old_shape(n):
        return (n, mats, piece, cols)

    def swap(value, mask):
        return exchange(value, mask, count)

    momentum = momentum.reshape(slots, 8, piece, cols)
    mine, other, odd = pl.pallas_call(
        first_kernel,
        in_specs=[pl.BlockSpec(memory_space=pltpu.HBM)] * 5,
        out_shape=[sds((half, mats * rows), F32)] * 2 + [sds(old_shape(4), BF16)],
        scratch_shapes=[
            pltpu.SMEM((mats,), jnp.int32),
            pltpu.VMEM((mats, rows, cols), F32),
            pltpu.VMEM((mats, rows, cols), BF16),
            pltpu.VMEM((mats, rank, cols), F32),
            pltpu.VMEM((slots, 8, piece, cols), BF16),
            pltpu.VMEM((2, half, rows), F32),
            pltpu.SemaphoreType.DMA((mats, 3)),
            pltpu.SemaphoreType.DMA((2,)),
        ],
        compiler_params=pltpu.CompilerParams(vmem_limit_bytes=40 * 1024 * 1024),
        name="first",
    )(*(pltpu.with_memory_space_constraint(v, pltpu.HBM) for v in (owners, grads, errs, q_t, momentum)))

    got = swap(odd, 1)
    mine = mine + swap(other, 1)
    evens = pl.pallas_call(
        even_kernel,
        grid=(1,),
        in_specs=[SMEM, whole((slots, 8, piece, cols)), whole(old_shape(4))],
        out_specs=[whole(old_shape(1))] * 4,
        out_shape=[sds(old_shape(1), BF16)] * 4,
        compiler_params=params(),
        name="even",
    )(owners, momentum, after(got, mine))
    got = [swap(evens[n], 2 * n) for n in (1, 2, 3)]
    mine = total_over(mine, bits[3:4], count)
    mine = after(mine, *evens)
    for bit in bits[4:]:
        mine = total_over(mine, [bit], count)
    old = after(evens[0], mine) + got[0] + got[1] + got[2]
    mine = after(mine, old)
    from_other = swap(old, 1 << bits[3])
    mine = total_over(mine, bits[1:3], count)
    old = after(old, mine) + from_other
    other = swap(mine, 1)

    right_all, keep, send2, send = pl.pallas_call(
        right_kernel,
        grid=(mats,),
        in_specs=[whole((half, mats * rows))] * 2 + [grad_spec, grad_spec],
        out_specs=[
            per_matrix((rank, cols)),
            per_matrix((quarter, cols)),
            per_matrix((quarter, cols)),
            pl.BlockSpec((2, 1, quarter, cols), lambda i: (0, i, 0, 0)),
        ],
        out_shape=[
            sds((mats, rank, cols), F32),
            sds((mats, quarter, cols), F32),
            sds((mats, quarter, cols), F32),
            sds((2, mats, quarter, cols), F32),
        ],
        scratch_shapes=[pltpu.VMEM((mats, 2, half, rows), F32), pltpu.VMEM((4, quarter, cols), F32)],
        compiler_params=params(),
        name="right",
    )(mine, other, grads, errs)

    w = pl.pallas_call(
        solve_kernel,
        grid=(1,),
        in_specs=[whole((half, mats * rows))] * 2,
        out_specs=whole((mats, rows, 3 * rank)),
        out_shape=sds((mats, rows, 3 * rank), BF16),
        scratch_shapes=[pltpu.VMEM((mats, 2, half, rows), F32)],
        compiler_params=params(),
        cost_estimate=cost(16),
        name="solve",
    )(mine, other)

    got = swap(after(send, old), 1)
    for bit in bits[4:-1]:
        old = old + swap(old, 1 << bit)
    from_other = swap(old, 1 << bits[-1])
    r0 = keep + got[0] + swap(send2 + got[1], 2)
    r0 = total_over(r0, bits[2:3], count)
    old = after(old, r0, w) + from_other
    r0 = after(r0, old)
    near = [swap(old, 2), swap(old, 4)]
    for n, bit in enumerate(bits[3:]):
        r0 = total_over(r0, [bit], count)
        if n == 0:
            near = [after(value, r0) for value in near]
            r0 = after(r0, *near)
    far = swap(near[0], 4)
    evens = jnp.concatenate([after(old, r0)] + near + [far])
    odds = swap(evens, 1)
    r1, r2, r3 = (swap(r0, mask) for mask in (1, 2, 3))
    new_errors = pl.pallas_call(
        error_kernel,
        grid=(mats,),
        in_specs=[grad_spec, grad_spec, per_matrix((rows, 3 * rank)), per_matrix((rank, cols))],
        out_specs=grad_spec,
        out_shape=sds((mats, rows, cols), BF16),
        compiler_params=params(),
        cost_estimate=cost(12),
        name="errors",
    )(grads, errs, after(w, evens), right_all)
    w = after(w, new_errors)

    quarter_spec = per_matrix((quarter, cols))
    old_spec = pl.BlockSpec((4, 1, piece, cols), lambda i: (0, i, 0, 0))
    steps, new_mom = pl.pallas_call(
        step_kernel,
        grid=(mats,),
        in_specs=[SMEM] * 4 + [quarter_spec] * 4 + [per_matrix((rows, 3 * rank))] + [old_spec] * 2,
        out_specs=[per_matrix((8, piece, cols)), whole((slots, 8, piece, cols))],
        out_shape=[sds((mats, 8, piece, cols), BF16), sds((slots, 8, piece, cols), BF16)],
        scratch_shapes=[pltpu.VMEM((4, quarter, cols), F32), pltpu.VMEM((8, piece, cols), F32)],
        compiler_params=params(),
        name="step",
    )(owners, buckets, learn_rates, beta_values, r0, r1, r2, r3, w, evens, odds)
    return (new_errors[None], steps.reshape(1, mats, rows, cols), new_mom.reshape(slots, rows, cols))


def solution(mesh):
    count = mesh.shape["dp"] * mesh.shape["group"]
    rep = P(AXES, None, None, None)
    return jax.shard_map(
        functools.partial(on_device, count),
        mesh=mesh,
        in_specs=(rep, rep, P(), P(), P(), P(), P(), P(AXES, None, None)),
        out_specs=(rep, rep, P(AXES, None, None)),
        check_vma=False,
    )
```

```python
import functools

import jax
import jax.numpy as jnp
from jax import lax
from jax.experimental import pallas as pl
from jax.experimental.pallas import tpu as pltpu
from jax.sharding import PartitionSpec as P

AXES = ("dp", "group")
F32 = jnp.float32
BF16 = jnp.bfloat16
SMEM = pl.BlockSpec(memory_space=pltpu.SMEM)


def whole(shape):
    return pl.BlockSpec(shape, lambda i: (0,) * len(shape))


def per_matrix(shape):
    return pl.BlockSpec((1,) + shape, lambda i: (i,) + (0,) * len(shape))


def split(value):
    high = value.astype(BF16)
    return high, (value - high.astype(F32)).astype(BF16)


def dot(left, right, dims):
    return lax.dot_general(left, right, (dims, ((), ())), preferred_element_type=F32)


def params(mebibytes=40):
    return pltpu.CompilerParams(dimension_semantics=("arbitrary",), vmem_limit_bytes=mebibytes * 1024 * 1024)


def cost(mebibytes):
    return pl.CostEstimate(flops=0, transcendentals=0, bytes_accessed=mebibytes * 1024 * 1024)


def after(value, *others):
    return lax.optimization_barrier((value,) + others)[0]


def gather_left(mine_ref, other_ref, left_ref, rows):
    bit = lax.axis_index(AXES) & 1
    for m in range(left_ref.shape[0]):
        left_ref[m, bit] = mine_ref[:, m * rows : (m + 1) * rows]
        left_ref[m, 1 - bit] = other_ref[:, m * rows : (m + 1) * rows]


def right_kernel(mine_ref, other_ref, grad_ref, error_ref, all_ref, k0_ref, k2_ref, s1_ref, s3_ref, left_ref, right_ref):
    i = pl.program_id(0)
    low_bits = lax.axis_index(AXES) & 3
    rows = grad_ref.shape[1]

    @pl.when(i == 0)
    def _():
        gather_left(mine_ref, other_ref, left_ref, rows)

    merged = grad_ref[0] + error_ref[0].astype(F32)
    high, low = split(merged)
    left = left_ref[i].reshape(-1, rows)
    rank = left.shape[0]
    l_both = jnp.concatenate(split(left), 0)
    both = dot(l_both, high, ((1,), (0,))) + dot(l_both, low, ((1,), (0,)))
    total = both[:rank] + both[rank:]
    all_ref[0] = total
    right_ref[...] = total.reshape(right_ref.shape)
    k0_ref[0] = right_ref[low_bits]
    k2_ref[0] = right_ref[low_bits ^ 2]
    s1_ref[0] = right_ref[low_bits ^ 1]
    s3_ref[0] = right_ref[low_bits ^ 3]


def three(left):
    high, low = split(left)
    return jnp.concatenate([high, high, low], 0)


def three_right(right):
    high, low = split(right)
    return jnp.concatenate([high, low, high], 0)


def solve_kernel(mine_ref, other_ref, w_ref, left_ref):
    mats, _, half, rows = left_ref.shape
    rank = 2 * half
    gather_left(mine_ref, other_ref, left_ref, rows)
    left = left_ref[...].reshape(mats, rank, rows)

    def exact(x, y, contract):
        return jnp.stack(
            [
                lax.dot_general(
                    x[m], y[m], (contract, ((), ())), precision=lax.Precision.HIGHEST, preferred_element_type=F32
                )
                for m in range(mats)
            ]
        )

    gram = exact(left, left, ((1,), (1,)))
    line = lax.broadcasted_iota(jnp.int32, gram.shape, 1)
    lane = lax.broadcasted_iota(jnp.int32, gram.shape, 2)
    for k in range(rank):
        inverse = 1.0 / gram[:, k : k + 1, k : k + 1]
        row = jnp.where(lane[:, k : k + 1] == k, inverse, gram[:, k : k + 1] * inverse)
        rest = jnp.where(lane == k, 0.0, gram) - gram[:, :, k : k + 1] * row
        gram = jnp.where(line == k, row, rest)
    solved = exact(gram, left, ((1,), (0,)))
    for m in range(mats):
        w_ref[m] = three(solved[m]).T


def error_kernel(grad_ref, error_ref, w_ref, all_ref, new_ref):
    approx = dot(w_ref[0], three_right(all_ref[0]), ((1,), (0,)))
    new_ref[0] = (grad_ref[0] + error_ref[0].astype(F32) - approx).astype(BF16)


def slot_of(owners_ref, i):
    slot = jnp.int32(0)
    for j in range(owners_ref.shape[0]):
        slot += jnp.where((j < i) & (owners_ref[j] == owners_ref[i]), 1, 0).astype(jnp.int32)
    return slot


def first_kernel(
    owners_hbm, grad_hbm, error_hbm, q_hbm, mom_hbm,
    mine_ref, other_ref, odd_ref,
    owners_ref, grad_ref, error_ref, q_ref, mom_ref, left_ref, sems, mom_sems,
):
    mats, rows, _ = grad_ref.shape
    rank = q_ref.shape[1]
    me = lax.axis_index(AXES)
    pairs = ((grad_hbm, grad_ref), (error_hbm, error_ref), (q_hbm, q_ref))
    copies = [
        [pltpu.make_async_copy(hbm.at[m], ref.at[m], sems.at[m, n]) for n, (hbm, ref) in enumerate(pairs)]
        for m in range(mats)
    ]
    mom_copies = [
        pltpu.make_async_copy(mom_hbm, mom_ref, mom_sems.at[0]),
        pltpu.make_async_copy(owners_hbm, owners_ref, mom_sems.at[1]),
    ]
    for copy in copies[0] + mom_copies:
        copy.start()

    odd_ref[...] = jnp.zeros(odd_ref.shape, BF16)
    for m in range(mats):
        if m + 1 < mats:
            for copy in copies[m + 1]:
                copy.start()
        for copy in copies[m]:
            copy.wait()
        high, low = split(grad_ref[m] + error_ref[m].astype(F32))
        q_both = jnp.concatenate(split(q_ref[m]), 0)
        both = dot(q_both, high, ((1,), (1,))) + dot(q_both, low, ((1,), (1,)))
        left_ref[...] = (both[:rank] + both[rank:]).reshape(left_ref.shape)
        mine_ref[:, m * rows : (m + 1) * rows] = left_ref[me & 1]
        other_ref[:, m * rows : (m + 1) * rows] = left_ref[1 - (me & 1)]
        if m == 0:
            for copy in mom_copies:
                copy.wait()
            for i in range(mats):
                slot = slot_of(owners_ref, i)

                @pl.when(owners_ref[i] == me)
                def _():
                    for n in range(4):
                        odd_ref[n, i] = mom_ref[slot, (2 * n + 1) ^ (me & 7)]


def even_kernel(owners_ref, mom_ref, got_ref, *outs):
    me = lax.axis_index(AXES)
    for n, out in enumerate(outs):
        out[0] = got_ref[n]
    for i in range(owners_ref.shape[0]):
        slot = slot_of(owners_ref, i)

        @pl.when(owners_ref[i] == me)
        def _():
            for n, out in enumerate(outs):
                out[0, i] = mom_ref[slot, (2 * n) ^ (me & 7)]


def step_kernel(
    owners_ref, buckets_ref, rates_ref, betas_ref,
    r0_ref, r1_ref, r2_ref, r3_ref, w_ref, even_ref, odd_ref,
    step_ref, mom_ref, right_ref, update_ref,
):
    i = pl.program_id(0)
    me = lax.axis_index(AXES)
    rate = rates_ref[buckets_ref[i]]
    beta = betas_ref[buckets_ref[i]]
    of_update, of_old = -rate * (1.0 + beta), -rate * beta * beta

    @pl.when(i == 0)
    def _():
        mom_ref[...] = jnp.zeros_like(mom_ref)

    for position, ref in enumerate((r0_ref, r1_ref, r2_ref, r3_ref)):
        right_ref[position ^ (me & 3)] = ref[0]
    right = three_right(right_ref[...].reshape(-1, right_ref.shape[2]))
    update_ref[...] = dot(w_ref[0], right, ((1,), (0,))).reshape(update_ref.shape)
    own = owners_ref[i] == me
    slot = slot_of(owners_ref, i)
    for position in range(8):
        ref = (even_ref, odd_ref)[position % 2]
        piece = position ^ (me & 7)
        update = update_ref[piece]
        old = ref[position // 2, 0].astype(F32)
        step_ref[0, piece] = (of_update * update + of_old * old).astype(BF16)

        @pl.when(own)
        def _():
            mom_ref[slot, piece] = (beta * old + update).astype(BF16)


def exchange(value, mask, count):
    return lax.ppermute(value, AXES, [(d, d ^ mask) for d in range(count)])


def total_over(value, bits, count):
    while bits:
        head, bits = bits[:2], bits[2:]
        masks = [1 << head[0]] if len(head) == 1 else [1 << head[0], 1 << head[1], (1 << head[0]) | (1 << head[1])]
        value = functools.reduce(jnp.add, [exchange(value, m, count) for m in masks], value)
    return value


def on_device(count, gradients, errors, q_init, owners, buckets, learn_rates, beta_values, momentum):
    grads, errs = gradients[0], errors[0]
    mats, rows, cols = grads.shape
    rank = q_init.shape[2]
    slots = momentum.shape[0]
    bits = list(range(count.bit_length() - 1))
    q_t = jnp.swapaxes(q_init, 1, 2)
    half, quarter, piece = rank // 2, rank // 4, rows // 8
    grad_spec = per_matrix((rows, cols))
    sds = jax.ShapeDtypeStruct

    def old_shape(n):
        return (n, mats, piece, cols)

    def swap(value, mask):
        return exchange(value, mask, count)

    momentum = momentum.reshape(slots, 8, piece, cols)
    mine, other, odd = pl.pallas_call(
        first_kernel,
        in_specs=[pl.BlockSpec(memory_space=pltpu.HBM)] * 5,
        out_shape=[sds((half, mats * rows), F32)] * 2 + [sds(old_shape(4), BF16)],
        scratch_shapes=[
            pltpu.SMEM((mats,), jnp.int32),
            pltpu.VMEM((mats, rows, cols), F32),
            pltpu.VMEM((mats, rows, cols), BF16),
            pltpu.VMEM((mats, rank, cols), F32),
            pltpu.VMEM((slots, 8, piece, cols), BF16),
            pltpu.VMEM((2, half, rows), F32),
            pltpu.SemaphoreType.DMA((mats, 3)),
            pltpu.SemaphoreType.DMA((2,)),
        ],
        compiler_params=pltpu.CompilerParams(vmem_limit_bytes=40 * 1024 * 1024),
        name="first",
    )(*(pltpu.with_memory_space_constraint(v, pltpu.HBM) for v in (owners, grads, errs, q_t, momentum)))

    got = swap(odd, 1)
    mine = mine + swap(other, 1)
    evens = pl.pallas_call(
        even_kernel,
        grid=(1,),
        in_specs=[SMEM, whole((slots, 8, piece, cols)), whole(old_shape(4))],
        out_specs=[whole(old_shape(1))] * 4,
        out_shape=[sds(old_shape(1), BF16)] * 4,
        compiler_params=params(),
        name="even",
    )(owners, momentum, after(got, mine))
    got = [swap(evens[n], 2 * n) for n in (1, 2, 3)]
    mine = total_over(mine, bits[3:4], count)
    mine = after(mine, *evens)
    for bit in bits[4:]:
        mine = total_over(mine, [bit], count)
    old = after(evens[0], mine) + got[0] + got[1] + got[2]
    mine = after(mine, old)
    from_other = swap(old, 1 << bits[-1])
    for bit in bits[1:3]:
        mine = total_over(mine, [bit], count)
    other = swap(mine, 1)

    right_all, keep, send2, send1, send3 = pl.pallas_call(
        right_kernel,
        grid=(mats,),
        in_specs=[whole((half, mats * rows))] * 2 + [grad_spec, grad_spec],
        out_specs=[per_matrix((rank, cols))] + [per_matrix((quarter, cols))] * 4,
        out_shape=[sds((mats, rank, cols), F32)] + [sds((mats, quarter, cols), F32)] * 4,
        scratch_shapes=[pltpu.VMEM((mats, 2, half, rows), F32), pltpu.VMEM((4, quarter, cols), F32)],
        compiler_params=params(),
        name="right",
    )(mine, other, grads, errs)

    w = pl.pallas_call(
        solve_kernel,
        grid=(1,),
        in_specs=[whole((half, mats * rows))] * 2,
        out_specs=whole((mats, rows, 3 * rank)),
        out_shape=sds((mats, rows, 3 * rank), BF16),
        scratch_shapes=[pltpu.VMEM((mats, 2, half, rows), F32)],
        compiler_params=params(),
        cost_estimate=cost(1),
        name="solve",
    )(mine, other)

    got = swap(send1, 1), swap(send3, 1)
    r0, send2 = keep + got[0], send2 + got[1]
    old = after(old, r0, send2) + from_other
    for bit in reversed(bits[4:-1]):
        old = old + swap(old, 1 << bit)
    send2 = after(send2, old)
    from_other = swap(old, 1 << bits[3])
    r0 = r0 + swap(send2, 2)
    r0 = total_over(r0, bits[2:3], count)
    old = after(old, r0, w) + from_other
    r0 = after(r0, old)
    near = [swap(old, 2), swap(old, 4)]
    for n, bit in enumerate(bits[3:]):
        r0 = total_over(r0, [bit], count)
        if n == 0:
            near = [after(value, r0) for value in near]
            r0 = after(r0, *near)
    far = swap(near[0], 4)
    evens = jnp.concatenate([after(old, r0)] + near + [far])
    odds = swap(evens, 1)
    r1, r2 = swap(r0, 1), swap(r0, 2)
    r3 = swap(r2, 1)
    new_errors = pl.pallas_call(
        error_kernel,
        grid=(mats,),
        in_specs=[grad_spec, grad_spec, per_matrix((rows, 3 * rank)), per_matrix((rank, cols))],
        out_specs=grad_spec,
        out_shape=sds((mats, rows, cols), BF16),
        compiler_params=params(),
        cost_estimate=cost(12),
        name="errors",
    )(grads, errs, after(w, evens), right_all)
    w = after(w, new_errors)

    quarter_spec = per_matrix((quarter, cols))
    old_spec = pl.BlockSpec((4, 1, piece, cols), lambda i: (0, i, 0, 0))
    steps, new_mom = pl.pallas_call(
        step_kernel,
        grid=(mats,),
        in_specs=[SMEM] * 4 + [quarter_spec] * 4 + [per_matrix((rows, 3 * rank))] + [old_spec] * 2,
        out_specs=[per_matrix((8, piece, cols)), whole((slots, 8, piece, cols))],
        out_shape=[sds((mats, 8, piece, cols), BF16), sds((slots, 8, piece, cols), BF16)],
        scratch_shapes=[pltpu.VMEM((4, quarter, cols), F32), pltpu.VMEM((8, piece, cols), F32)],
        compiler_params=params(),
        name="step",
    )(owners, buckets, learn_rates, beta_values, r0, r1, r2, r3, w, evens, odds)
    return (new_errors[None], steps.reshape(1, mats, rows, cols), new_mom.reshape(slots, rows, cols))


def solution(mesh):
    count = mesh.shape["dp"] * mesh.shape["group"]
    rep = P(AXES, None, None, None)
    return jax.shard_map(
        functools.partial(on_device, count),
        mesh=mesh,
        in_specs=(rep, rep, P(), P(), P(), P(), P(), P(AXES, None, None)),
        out_specs=(rep, rep, P(AXES, None, None)),
        check_vma=False,
    )
```

```python
import functools

import jax
import jax.numpy as jnp
from jax import lax
from jax.experimental import pallas as pl
from jax.experimental.pallas import tpu as pltpu
from jax.sharding import PartitionSpec as P

AXES = ("dp", "group")
F32 = jnp.float32
BF16 = jnp.bfloat16
SMEM = pl.BlockSpec(memory_space=pltpu.SMEM)


def whole(shape):
    return pl.BlockSpec(shape, lambda i: (0,) * len(shape))


def per_matrix(shape):
    return pl.BlockSpec((1,) + shape, lambda i: (i,) + (0,) * len(shape))


def split(value):
    high = value.astype(BF16)
    return high, (value - high.astype(F32)).astype(BF16)


def dot(left, right, dims):
    return lax.dot_general(left, right, (dims, ((), ())), preferred_element_type=F32)


def params(mebibytes=40):
    return pltpu.CompilerParams(dimension_semantics=("arbitrary",), vmem_limit_bytes=mebibytes * 1024 * 1024)


def cost(mebibytes):
    return pl.CostEstimate(flops=0, transcendentals=0, bytes_accessed=mebibytes * 1024 * 1024)


def after(value, *others):
    return lax.optimization_barrier((value,) + others)[0]


def gather_left(mine_ref, other_ref, left_ref, rows):
    bit = lax.axis_index(AXES) & 1
    for m in range(left_ref.shape[0]):
        left_ref[m, bit] = mine_ref[:, m * rows : (m + 1) * rows]
        left_ref[m, 1 - bit] = other_ref[:, m * rows : (m + 1) * rows]


def right_kernel(mine_ref, other_ref, grad_ref, error_ref, all_ref, k0_ref, k2_ref, s1_ref, s3_ref, left_ref, right_ref):
    i = pl.program_id(0)
    low_bits = lax.axis_index(AXES) & 3
    rows = grad_ref.shape[1]

    @pl.when(i == 0)
    def _():
        gather_left(mine_ref, other_ref, left_ref, rows)

    merged = grad_ref[0] + error_ref[0].astype(F32)
    high, low = split(merged)
    left = left_ref[i].reshape(-1, rows)
    rank = left.shape[0]
    l_both = jnp.concatenate(split(left), 0)
    both = dot(l_both, high, ((1,), (0,))) + dot(l_both, low, ((1,), (0,)))
    total = both[:rank] + both[rank:]
    all_ref[0] = total
    right_ref[...] = total.reshape(right_ref.shape)
    k0_ref[0] = right_ref[low_bits]
    k2_ref[0] = right_ref[low_bits ^ 2]
    s1_ref[0] = right_ref[low_bits ^ 1]
    s3_ref[0] = right_ref[low_bits ^ 3]


def three(left):
    high, low = split(left)
    return jnp.concatenate([high, high, low], 0)


def three_right(right):
    high, low = split(right)
    return jnp.concatenate([high, low, high], 0)


def solve_kernel(mine_ref, other_ref, w_ref, left_ref):
    mats, _, half, rows = left_ref.shape
    rank = 2 * half
    gather_left(mine_ref, other_ref, left_ref, rows)
    left = left_ref[...].reshape(mats, rank, rows)

    def exact(x, y, contract):
        return jnp.stack(
            [
                lax.dot_general(
                    x[m], y[m], (contract, ((), ())), precision=lax.Precision.HIGHEST, preferred_element_type=F32
                )
                for m in range(mats)
            ]
        )

    gram = exact(left, left, ((1,), (1,)))
    line = lax.broadcasted_iota(jnp.int32, gram.shape, 1)
    lane = lax.broadcasted_iota(jnp.int32, gram.shape, 2)
    for k in range(rank):
        inverse = 1.0 / gram[:, k : k + 1, k : k + 1]
        row = jnp.where(lane[:, k : k + 1] == k, inverse, gram[:, k : k + 1] * inverse)
        rest = jnp.where(lane == k, 0.0, gram) - gram[:, :, k : k + 1] * row
        gram = jnp.where(line == k, row, rest)
    solved = exact(gram, left, ((1,), (0,)))
    for m in range(mats):
        w_ref[m] = three(solved[m]).T


def error_kernel(grad_ref, error_ref, w_ref, all_ref, new_ref):
    approx = dot(w_ref[0], three_right(all_ref[0]), ((1,), (0,)))
    new_ref[0] = (grad_ref[0] + error_ref[0].astype(F32) - approx).astype(BF16)


def slot_of(owners_ref, i):
    slot = jnp.int32(0)
    for j in range(owners_ref.shape[0]):
        slot += jnp.where((j < i) & (owners_ref[j] == owners_ref[i]), 1, 0).astype(jnp.int32)
    return slot


def first_kernel(
    owners_hbm, grad_hbm, error_hbm, q_hbm, mom_hbm,
    mine_ref, other_ref, odd_ref,
    owners_ref, grad_ref, error_ref, q_ref, mom_ref, left_ref, sems, mom_sems,
):
    mats, rows, _ = grad_ref.shape
    rank = q_ref.shape[1]
    me = lax.axis_index(AXES)
    pairs = ((grad_hbm, grad_ref), (error_hbm, error_ref), (q_hbm, q_ref))
    copies = [
        [pltpu.make_async_copy(hbm.at[m], ref.at[m], sems.at[m, n]) for n, (hbm, ref) in enumerate(pairs)]
        for m in range(mats)
    ]
    mom_copies = [
        pltpu.make_async_copy(mom_hbm, mom_ref, mom_sems.at[0]),
        pltpu.make_async_copy(owners_hbm, owners_ref, mom_sems.at[1]),
    ]
    for copy in copies[0] + mom_copies:
        copy.start()

    odd_ref[...] = jnp.zeros(odd_ref.shape, BF16)
    for m in range(mats):
        if m + 1 < mats:
            for copy in copies[m + 1]:
                copy.start()
        for copy in copies[m]:
            copy.wait()
        high, low = split(grad_ref[m] + error_ref[m].astype(F32))
        q_both = jnp.concatenate(split(q_ref[m]), 0)
        both = dot(q_both, high, ((1,), (1,))) + dot(q_both, low, ((1,), (1,)))
        left_ref[...] = (both[:rank] + both[rank:]).reshape(left_ref.shape)
        mine_ref[:, m * rows : (m + 1) * rows] = left_ref[me & 1]
        other_ref[:, m * rows : (m + 1) * rows] = left_ref[1 - (me & 1)]
        if m == 0:
            for copy in mom_copies:
                copy.wait()
            for i in range(mats):
                slot = slot_of(owners_ref, i)

                @pl.when(owners_ref[i] == me)
                def _():
                    for n in range(4):
                        odd_ref[n, i] = mom_ref[slot, (2 * n + 1) ^ (me & 7)]


def even_kernel(owners_ref, mom_ref, got_ref, *outs):
    me = lax.axis_index(AXES)
    for n, out in enumerate(outs):
        out[0] = got_ref[n]
    for i in range(owners_ref.shape[0]):
        slot = slot_of(owners_ref, i)

        @pl.when(owners_ref[i] == me)
        def _():
            for n, out in enumerate(outs):
                out[0, i] = mom_ref[slot, (2 * n) ^ (me & 7)]


def step_kernel(
    owners_ref, buckets_ref, rates_ref, betas_ref,
    r0_ref, r1_ref, r2_ref, r3_ref, w_ref, even_ref, odd_ref, far_ref, odd_far_ref,
    step_ref, mom_ref, right_ref, update_ref,
):
    i = pl.program_id(0)
    me = lax.axis_index(AXES)
    rate = rates_ref[buckets_ref[i]]
    beta = betas_ref[buckets_ref[i]]
    of_update, of_old = -rate * (1.0 + beta), -rate * beta * beta

    @pl.when(i == 0)
    def _():
        mom_ref[...] = jnp.zeros_like(mom_ref)

    for position, ref in enumerate((r0_ref, r1_ref, r2_ref, r3_ref)):
        right_ref[position ^ (me & 3)] = ref[0]
    right = three_right(right_ref[...].reshape(-1, right_ref.shape[2]))
    update_ref[...] = dot(w_ref[0], right, ((1,), (0,))).reshape(update_ref.shape)
    own = owners_ref[i] == me
    slot = slot_of(owners_ref, i)
    for position in range(8):
        near, far = ((even_ref, far_ref), (odd_ref, odd_far_ref))[position % 2]
        piece = position ^ (me & 7)
        update = update_ref[piece]
        old = (near[position // 2, 0] if position < 6 else far[0, 0]).astype(F32)
        step_ref[0, piece] = (of_update * update + of_old * old).astype(BF16)

        @pl.when(own)
        def _():
            mom_ref[slot, piece] = (beta * old + update).astype(BF16)


def exchange(value, mask, count):
    return lax.ppermute(value, AXES, [(d, d ^ mask) for d in range(count)])


def total_over(value, bits, count):
    while bits:
        head, bits = bits[:2], bits[2:]
        masks = [1 << head[0]] if len(head) == 1 else [1 << head[0], 1 << head[1], (1 << head[0]) | (1 << head[1])]
        value = functools.reduce(jnp.add, [exchange(value, m, count) for m in masks], value)
    return value


def on_device(count, gradients, errors, q_init, owners, buckets, learn_rates, beta_values, momentum):
    grads, errs = gradients[0], errors[0]
    mats, rows, cols = grads.shape
    rank = q_init.shape[2]
    slots = momentum.shape[0]
    bits = list(range(count.bit_length() - 1))
    q_t = jnp.swapaxes(q_init, 1, 2)
    half, quarter, piece = rank // 2, rank // 4, rows // 8
    grad_spec = per_matrix((rows, cols))
    sds = jax.ShapeDtypeStruct

    def old_shape(n):
        return (n, mats, piece, cols)

    def swap(value, mask):
        return exchange(value, mask, count)

    momentum = momentum.reshape(slots, 8, piece, cols)
    mine, other, odd = pl.pallas_call(
        first_kernel,
        in_specs=[pl.BlockSpec(memory_space=pltpu.HBM)] * 5,
        out_shape=[sds((half, mats * rows), F32)] * 2 + [sds(old_shape(4), BF16)],
        scratch_shapes=[
            pltpu.SMEM((mats,), jnp.int32),
            pltpu.VMEM((mats, rows, cols), F32),
            pltpu.VMEM((mats, rows, cols), BF16),
            pltpu.VMEM((mats, rank, cols), F32),
            pltpu.VMEM((slots, 8, piece, cols), BF16),
            pltpu.VMEM((2, half, rows), F32),
            pltpu.SemaphoreType.DMA((mats, 3)),
            pltpu.SemaphoreType.DMA((2,)),
        ],
        compiler_params=pltpu.CompilerParams(vmem_limit_bytes=40 * 1024 * 1024),
        name="first",
    )(*(pltpu.with_memory_space_constraint(v, pltpu.HBM) for v in (owners, grads, errs, q_t, momentum)))

    got = swap(odd, 1)
    mine = mine + swap(other, 1)
    evens = pl.pallas_call(
        even_kernel,
        grid=(1,),
        in_specs=[SMEM, whole((slots, 8, piece, cols)), whole(old_shape(4))],
        out_specs=[whole(old_shape(1))] * 4,
        out_shape=[sds(old_shape(1), BF16)] * 4,
        compiler_params=params(),
        name="even",
    )(owners, momentum, after(got, mine))
    got = [swap(evens[n], 2 * n) for n in (1, 2, 3)]
    mine = total_over(mine, bits[3:4], count)
    mine = after(mine, *evens)
    for bit in bits[4:]:
        mine = total_over(mine, [bit], count)
    old = after(evens[0], mine) + got[0] + got[1] + got[2]
    mine = after(mine, old)
    from_other = swap(old, 1 << bits[-1])
    for bit in bits[1:3]:
        mine = total_over(mine, [bit], count)
    other = swap(mine, 1)

    right_all, keep, send2, send1, send3 = pl.pallas_call(
        right_kernel,
        grid=(mats,),
        in_specs=[whole((half, mats * rows))] * 2 + [grad_spec, grad_spec],
        out_specs=[per_matrix((rank, cols))] + [per_matrix((quarter, cols))] * 4,
        out_shape=[sds((mats, rank, cols), F32)] + [sds((mats, quarter, cols), F32)] * 4,
        scratch_shapes=[pltpu.VMEM((mats, 2, half, rows), F32), pltpu.VMEM((4, quarter, cols), F32)],
        compiler_params=params(),
        name="right",
    )(mine, other, grads, errs)

    w = pl.pallas_call(
        solve_kernel,
        grid=(1,),
        in_specs=[whole((half, mats * rows))] * 2,
        out_specs=whole((mats, rows, 3 * rank)),
        out_shape=sds((mats, rows, 3 * rank), BF16),
        scratch_shapes=[pltpu.VMEM((mats, 2, half, rows), F32)],
        compiler_params=params(),
        cost_estimate=cost(1),
        name="solve",
    )(mine, other)

    got = swap(send1, 1), swap(send3, 1)
    r0, send2 = keep + got[0], send2 + got[1]
    old = after(old, r0, send2) + from_other
    for bit in reversed(bits[4:-1]):
        old = old + swap(old, 1 << bit)
    send2 = after(send2, old)
    from_other = swap(old, 1 << bits[3])
    r0 = r0 + swap(send2, 2)
    r0 = total_over(r0, bits[2:3], count)
    old = after(old, r0, w) + from_other
    r0 = after(r0, old)
    near = [swap(old, 2), swap(old, 4)]
    for n, bit in enumerate(bits[3:]):
        r0 = total_over(r0, [bit], count)
        if n == 0:
            near = [after(value, r0) for value in near]
            r0 = after(r0, *near)
    far = swap(near[0], 4)
    new_errors = pl.pallas_call(
        error_kernel,
        grid=(mats,),
        in_specs=[grad_spec, grad_spec, per_matrix((rows, 3 * rank)), per_matrix((rank, cols))],
        out_specs=grad_spec,
        out_shape=sds((mats, rows, cols), BF16),
        compiler_params=params(),
        cost_estimate=cost(12),
        name="errors",
    )(grads, errs, after(w, *near), right_all)
    r0 = after(r0, new_errors)
    r1, r2 = swap(r0, 1), swap(r0, 2)
    evens = jnp.concatenate([old] + near)
    odds = swap(evens, 1)
    r3 = swap(r2, 1)
    far = after(far, r0)
    odd_far = swap(far, 1)

    quarter_spec = per_matrix((quarter, cols))
    old_specs = [pl.BlockSpec((n, 1, piece, cols), lambda i: (0, i, 0, 0)) for n in (3, 3, 1, 1)]
    steps, new_mom = pl.pallas_call(
        step_kernel,
        grid=(mats,),
        in_specs=[SMEM] * 4 + [quarter_spec] * 4 + [per_matrix((rows, 3 * rank))] + old_specs,
        out_specs=[per_matrix((8, piece, cols)), whole((slots, 8, piece, cols))],
        out_shape=[sds((mats, 8, piece, cols), BF16), sds((slots, 8, piece, cols), BF16)],
        scratch_shapes=[pltpu.VMEM((4, quarter, cols), F32), pltpu.VMEM((8, piece, cols), F32)],
        compiler_params=params(),
        name="step",
    )(owners, buckets, learn_rates, beta_values, r0, r1, r2, r3, w, evens, odds, far, odd_far)
    return (new_errors[None], steps.reshape(1, mats, rows, cols), new_mom.reshape(slots, rows, cols))


def solution(mesh):
    count = mesh.shape["dp"] * mesh.shape["group"]
    rep = P(AXES, None, None, None)
    return jax.shard_map(
        functools.partial(on_device, count),
        mesh=mesh,
        in_specs=(rep, rep, P(), P(), P(), P(), P(), P(AXES, None, None)),
        out_specs=(rep, rep, P(AXES, None, None)),
        check_vma=False,
    )
```

```python
import functools

import jax
import jax.numpy as jnp
from jax import lax
from jax.experimental import pallas as pl
from jax.experimental.pallas import tpu as pltpu
from jax.sharding import PartitionSpec as P

AXES = ("dp", "group")
F32 = jnp.float32
BF16 = jnp.bfloat16
SMEM = pl.BlockSpec(memory_space=pltpu.SMEM)
VMEM = pl.BlockSpec(memory_space=pltpu.VMEM)
ANY = pl.BlockSpec(memory_space=pl.ANY)


def whole(shape):
    return pl.BlockSpec(shape, lambda i: (0,) * len(shape))


def per_matrix(shape):
    return pl.BlockSpec((1,) + shape, lambda i: (i,) + (0,) * len(shape))


def split(value):
    high = value.astype(BF16)
    return high, (value - high.astype(F32)).astype(BF16)


def dot(left, right, dims):
    return lax.dot_general(left, right, (dims, ((), ())), preferred_element_type=F32)


def params(mebibytes=40):
    return pltpu.CompilerParams(dimension_semantics=("arbitrary",), vmem_limit_bytes=mebibytes * 1024 * 1024)


def cost(mebibytes):
    return pl.CostEstimate(flops=0, transcendentals=0, bytes_accessed=mebibytes * 1024 * 1024)


def after(value, *others):
    return lax.optimization_barrier((value,) + others)[0]


def gather_left(mine_ref, other_ref, left_ref, rows):
    bit = lax.axis_index(AXES) & 1
    for m in range(left_ref.shape[0]):
        left_ref[m, bit] = mine_ref[:, m * rows : (m + 1) * rows]
        left_ref[m, 1 - bit] = other_ref[:, m * rows : (m + 1) * rows]


def right_kernel(
    mine_ref, other_ref, grad_ref, error_ref, all_ref, k0_ref, k2_ref, s1_ref, s3_ref, left_ref, right_ref
):
    low_bits = lax.axis_index(AXES) & 3
    mats, rows, _ = grad_ref.shape
    gather_left(mine_ref, other_ref, left_ref, rows)
    for m in range(mats):
        high, low = split(grad_ref[m] + error_ref[m].astype(F32))
        left = left_ref[m].reshape(-1, rows)
        rank = left.shape[0]
        l_both = jnp.concatenate(split(left), 0)
        both = dot(l_both, high, ((1,), (0,))) + dot(l_both, low, ((1,), (0,)))
        total = both[:rank] + both[rank:]
        all_ref[m] = total
        right_ref[...] = total.reshape(right_ref.shape)
        k0_ref[m] = right_ref[low_bits]
        k2_ref[m] = right_ref[low_bits ^ 2]
        s1_ref[m] = right_ref[low_bits ^ 1]
        s3_ref[m] = right_ref[low_bits ^ 3]


def three(left):
    high, low = split(left)
    return jnp.concatenate([high, high, low], 0)


def three_right(right):
    high, low = split(right)
    return jnp.concatenate([high, low, high], 0)


def solve_kernel(mine_ref, other_ref, w_ref, left_ref):
    mats, _, half, rows = left_ref.shape
    rank = 2 * half
    gather_left(mine_ref, other_ref, left_ref, rows)
    left = left_ref[...].reshape(mats, rank, rows)

    def exact(x, y, contract):
        return jnp.stack(
            [
                lax.dot_general(
                    x[m], y[m], (contract, ((), ())), precision=lax.Precision.HIGHEST, preferred_element_type=F32
                )
                for m in range(mats)
            ]
        )

    gram = exact(left, left, ((1,), (1,)))
    line = lax.broadcasted_iota(jnp.int32, gram.shape, 1)
    lane = lax.broadcasted_iota(jnp.int32, gram.shape, 2)
    for k in range(rank):
        inverse = 1.0 / gram[:, k : k + 1, k : k + 1]
        row = jnp.where(lane[:, k : k + 1] == k, inverse, gram[:, k : k + 1] * inverse)
        rest = jnp.where(lane == k, 0.0, gram) - gram[:, :, k : k + 1] * row
        gram = jnp.where(line == k, row, rest)
    solved = exact(gram, left, ((1,), (0,)))
    for m in range(mats):
        w_ref[m] = three(solved[m]).T


def error_kernel(grad_ref, error_ref, w_ref, all_ref, new_ref):
    approx = dot(w_ref[0], three_right(all_ref[0]), ((1,), (0,)))
    new_ref[0] = (grad_ref[0] + error_ref[0].astype(F32) - approx).astype(BF16)


def slot_of(owners_ref, i):
    slot = jnp.int32(0)
    for j in range(owners_ref.shape[0]):
        slot += jnp.where((j < i) & (owners_ref[j] == owners_ref[i]), 1, 0).astype(jnp.int32)
    return slot


def first_kernel(
    owners_hbm, grad_hbm, error_hbm, q_hbm, mom_hbm,
    mine_ref, other_ref, odd_ref,
    owners_ref, grad_ref, error_ref, q_ref, mom_ref, left_ref, sems, mom_sems,
):
    mats, rows, _ = grad_ref.shape
    rank = q_ref.shape[1]
    me = lax.axis_index(AXES)
    pairs = ((grad_hbm, grad_ref), (error_hbm, error_ref), (q_hbm, q_ref))
    copies = [
        [pltpu.make_async_copy(hbm.at[m], ref.at[m], sems.at[m, n]) for n, (hbm, ref) in enumerate(pairs)]
        for m in range(mats)
    ]
    mom_copies = [
        pltpu.make_async_copy(mom_hbm, mom_ref, mom_sems.at[0]),
        pltpu.make_async_copy(owners_hbm, owners_ref, mom_sems.at[1]),
    ]
    for copy in copies[0] + mom_copies:
        copy.start()

    odd_ref[...] = jnp.zeros(odd_ref.shape, BF16)
    for m in range(mats):
        if m + 1 < mats:
            for copy in copies[m + 1]:
                copy.start()
        for copy in copies[m]:
            copy.wait()
        high, low = split(grad_ref[m] + error_ref[m].astype(F32))
        q_both = jnp.concatenate(split(q_ref[m]), 0)
        both = dot(q_both, high, ((1,), (1,))) + dot(q_both, low, ((1,), (1,)))
        left_ref[...] = (both[:rank] + both[rank:]).reshape(left_ref.shape)
        mine_ref[:, m * rows : (m + 1) * rows] = left_ref[me & 1]
        other_ref[:, m * rows : (m + 1) * rows] = left_ref[1 - (me & 1)]
        if m == 0:
            for copy in mom_copies:
                copy.wait()
            for i in range(mats):
                slot = slot_of(owners_ref, i)

                @pl.when(owners_ref[i] == me)
                def _():
                    for n in range(4):
                        odd_ref[n, i] = mom_ref[slot, (2 * n + 1) ^ (me & 7)]


def even_kernel(owners_ref, mom_ref, got_ref, *outs):
    me = lax.axis_index(AXES)
    for n, out in enumerate(outs):
        out[0] = got_ref[n]
    for i in range(owners_ref.shape[0]):
        slot = slot_of(owners_ref, i)

        @pl.when(owners_ref[i] == me)
        def _():
            for n, out in enumerate(outs):
                out[0, i] = mom_ref[slot, (2 * n) ^ (me & 7)]


def step_kernel(
    owners_ref, buckets_ref, rates_ref, betas_ref,
    r0_ref, r1_ref, r2_ref, r3_ref, w_ref, even_ref, odd_ref, far_ref, odd_far_ref,
    step_hbm, mom_hbm, step_ref, mom_ref, zero_ref, right_ref, update_ref, step_sems, mom_sems,
):
    me = lax.axis_index(AXES)
    mats, slots = step_ref.shape[0], mom_ref.shape[0]
    own = [owners_ref[m] == me for m in range(mats)]
    slot = [slot_of(owners_ref, m) for m in range(mats)]
    zero_ref[...] = jnp.zeros_like(zero_ref)
    for n in range(slots):
        used = jnp.bool_(False)
        for m in range(mats):
            used |= own[m] & (slot[m] == n)

        @pl.when(jnp.logical_not(used))
        def _():
            pltpu.make_async_copy(zero_ref, mom_hbm.at[n], mom_sems.at[n]).start()

    for m in range(mats):
        rate = rates_ref[buckets_ref[m]]
        beta = betas_ref[buckets_ref[m]]
        of_update, of_old = -rate * (1.0 + beta), -rate * beta * beta
        for position, ref in enumerate((r0_ref, r1_ref, r2_ref, r3_ref)):
            right_ref[position ^ (me & 3)] = ref[m]
        right = three_right(right_ref[...].reshape(-1, right_ref.shape[2]))
        update_ref[...] = dot(w_ref[m], right, ((1,), (0,))).reshape(update_ref.shape)
        for position in range(8):
            near, far = ((even_ref, far_ref), (odd_ref, odd_far_ref))[position % 2]
            piece = position ^ (me & 7)
            update = update_ref[piece]
            old = (near[position // 2, m] if position < 6 else far[0, m]).astype(F32)
            step_ref[m, piece] = (of_update * update + of_old * old).astype(BF16)

            @pl.when(own[m])
            def _():
                mom_ref[slot[m], piece] = (beta * old + update).astype(BF16)

        pltpu.make_async_copy(step_ref.at[m], step_hbm.at[m], step_sems.at[m]).start()

        @pl.when(own[m])
        def _():
            n = slot[m]
            pltpu.make_async_copy(mom_ref.at[n], mom_hbm.at[n], mom_sems.at[n]).start()

    for n in range(slots):
        pltpu.make_async_copy(zero_ref, mom_hbm.at[n], mom_sems.at[n]).wait()
    for m in range(mats):
        pltpu.make_async_copy(step_ref.at[m], step_hbm.at[m], step_sems.at[m]).wait()


def exchange(value, mask, count):
    return lax.ppermute(value, AXES, [(d, d ^ mask) for d in range(count)])


def total_over(value, bits, count):
    while bits:
        head, bits = bits[:2], bits[2:]
        masks = [1 << head[0]] if len(head) == 1 else [1 << head[0], 1 << head[1], (1 << head[0]) | (1 << head[1])]
        value = functools.reduce(jnp.add, [exchange(value, m, count) for m in masks], value)
    return value


def on_device(count, gradients, errors, q_init, owners, buckets, learn_rates, beta_values, momentum):
    grads, errs = gradients[0], errors[0]
    mats, rows, cols = grads.shape
    rank = q_init.shape[2]
    slots = momentum.shape[0]
    bits = list(range(count.bit_length() - 1))
    q_t = jnp.swapaxes(q_init, 1, 2)
    half, quarter, piece = rank // 2, rank // 4, rows // 8
    grad_spec = per_matrix((rows, cols))
    sds = jax.ShapeDtypeStruct

    def old_shape(n):
        return (n, mats, piece, cols)

    def swap(value, mask):
        return exchange(value, mask, count)

    momentum = momentum.reshape(slots, 8, piece, cols)
    mine, other, odd = pl.pallas_call(
        first_kernel,
        in_specs=[pl.BlockSpec(memory_space=pltpu.HBM)] * 5,
        out_shape=[sds((half, mats * rows), F32)] * 2 + [sds(old_shape(4), BF16)],
        scratch_shapes=[
            pltpu.SMEM((mats,), jnp.int32),
            pltpu.VMEM((mats, rows, cols), F32),
            pltpu.VMEM((mats, rows, cols), BF16),
            pltpu.VMEM((mats, rank, cols), F32),
            pltpu.VMEM((slots, 8, piece, cols), BF16),
            pltpu.VMEM((2, half, rows), F32),
            pltpu.SemaphoreType.DMA((mats, 3)),
            pltpu.SemaphoreType.DMA((2,)),
        ],
        compiler_params=pltpu.CompilerParams(vmem_limit_bytes=40 * 1024 * 1024),
        name="first",
    )(*(pltpu.with_memory_space_constraint(v, pltpu.HBM) for v in (owners, grads, errs, q_t, momentum)))

    got = swap(odd, 1)
    mine = mine + swap(other, 1)
    evens = pl.pallas_call(
        even_kernel,
        in_specs=[SMEM, VMEM, VMEM],
        out_specs=[VMEM] * 4,
        out_shape=[sds(old_shape(1), BF16)] * 4,
        compiler_params=pltpu.CompilerParams(vmem_limit_bytes=40 * 1024 * 1024),
        name="even",
    )(owners, momentum, after(got, mine))
    got = [swap(evens[n], 2 * n) for n in (1, 2, 3)]
    mine = total_over(mine, bits[3:4], count)
    mine = after(mine, *evens)
    for bit in bits[4:]:
        mine = total_over(mine, [bit], count)
    old = after(evens[0], mine) + got[0] + got[1] + got[2]
    mine = after(mine, old)
    from_other = swap(old, 1 << bits[-1])
    for bit in bits[1:3]:
        mine = total_over(mine, [bit], count)
    other = swap(mine, 1)

    right_all, keep, send2, send1, send3 = pl.pallas_call(
        right_kernel,
        in_specs=[VMEM] * 4,
        out_specs=[VMEM] * 5,
        out_shape=[sds((mats, rank, cols), F32)] + [sds((mats, quarter, cols), F32)] * 4,
        scratch_shapes=[pltpu.VMEM((mats, 2, half, rows), F32), pltpu.VMEM((4, quarter, cols), F32)],
        compiler_params=pltpu.CompilerParams(vmem_limit_bytes=40 * 1024 * 1024),
        name="right",
    )(mine, other, grads, errs)

    w = pl.pallas_call(
        solve_kernel,
        grid=(1,),
        in_specs=[whole((half, mats * rows))] * 2,
        out_specs=whole((mats, rows, 3 * rank)),
        out_shape=sds((mats, rows, 3 * rank), BF16),
        scratch_shapes=[pltpu.VMEM((mats, 2, half, rows), F32)],
        compiler_params=params(),
        cost_estimate=cost(1),
        name="solve",
    )(mine, other)

    got = swap(send1, 1), swap(send3, 1)
    r0, send2 = keep + got[0], send2 + got[1]
    old = after(old, r0, send2) + from_other
    for bit in reversed(bits[4:-1]):
        old = old + swap(old, 1 << bit)
    send2 = after(send2, old)
    from_other = swap(old, 1 << bits[3])
    r0 = r0 + swap(send2, 2)
    r0 = total_over(r0, bits[2:3], count)
    old = after(old, r0, w) + from_other
    r0 = after(r0, old)
    near = [swap(old, 2), swap(old, 4)]
    for n, bit in enumerate(bits[3:]):
        r0 = total_over(r0, [bit], count)
        if n == 0:
            near = [after(value, r0) for value in near]
            r0 = after(r0, *near)
    far = swap(near[0], 4)
    new_errors = pl.pallas_call(
        error_kernel,
        grid=(mats,),
        in_specs=[grad_spec, grad_spec, per_matrix((rows, 3 * rank)), per_matrix((rank, cols))],
        out_specs=grad_spec,
        out_shape=sds((mats, rows, cols), BF16),
        compiler_params=params(),
        cost_estimate=cost(12),
        name="errors",
    )(grads, errs, after(w, *near), right_all)
    r0 = after(r0, new_errors)
    r1, r2 = swap(r0, 1), swap(r0, 2)
    evens = jnp.concatenate([old] + near)
    odds = swap(evens, 1)
    r3 = swap(r2, 1)
    far = after(far, r0)
    odd_far = swap(after(far, r2), 1)

    pieces = (8, piece, cols)
    steps, new_mom = pl.pallas_call(
        step_kernel,
        in_specs=[SMEM] * 4 + [VMEM] * 9,
        out_specs=[ANY] * 2,
        out_shape=[sds((mats,) + pieces, BF16), sds((slots,) + pieces, BF16)],
        scratch_shapes=[
            pltpu.VMEM((mats,) + pieces, BF16),
            pltpu.VMEM((slots,) + pieces, BF16),
            pltpu.VMEM(pieces, BF16),
            pltpu.VMEM((4, quarter, cols), F32),
            pltpu.VMEM(pieces, F32),
            pltpu.SemaphoreType.DMA((mats,)),
            pltpu.SemaphoreType.DMA((slots,)),
        ],
        compiler_params=pltpu.CompilerParams(vmem_limit_bytes=40 * 1024 * 1024),
        name="step",
    )(owners, buckets, learn_rates, beta_values, r0, r1, r2, r3, w, evens, odds, far, odd_far)
    return (new_errors[None], steps.reshape(1, mats, rows, cols), new_mom.reshape(slots, rows, cols))


def solution(mesh):
    count = mesh.shape["dp"] * mesh.shape["group"]
    rep = P(AXES, None, None, None)
    return jax.shard_map(
        functools.partial(on_device, count),
        mesh=mesh,
        in_specs=(rep, rep, P(), P(), P(), P(), P(), P(AXES, None, None)),
        out_specs=(rep, rep, P(AXES, None, None)),
        check_vma=False,
    )
```

```python
import functools

import jax
import jax.numpy as jnp
from jax import lax
from jax.experimental import pallas as pl
from jax.experimental.pallas import tpu as pltpu
from jax.sharding import PartitionSpec as P

AXES = ("dp", "group")
F32 = jnp.float32
BF16 = jnp.bfloat16
SMEM = pl.BlockSpec(memory_space=pltpu.SMEM)
VMEM = pl.BlockSpec(memory_space=pltpu.VMEM)
ANY = pl.BlockSpec(memory_space=pl.ANY)


def whole(shape):
    return pl.BlockSpec(shape, lambda i: (0,) * len(shape))


def per_matrix(shape):
    return pl.BlockSpec((1,) + shape, lambda i: (i,) + (0,) * len(shape))


def split(value):
    high = value.astype(BF16)
    return high, (value - high.astype(F32)).astype(BF16)


def dot(left, right, dims):
    return lax.dot_general(left, right, (dims, ((), ())), preferred_element_type=F32)


def params(mebibytes=40):
    return pltpu.CompilerParams(dimension_semantics=("arbitrary",), vmem_limit_bytes=mebibytes * 1024 * 1024)


def cost(mebibytes):
    return pl.CostEstimate(flops=0, transcendentals=0, bytes_accessed=mebibytes * 1024 * 1024)


def after(value, *others):
    return lax.optimization_barrier((value,) + others)[0]


def gather_left(mine_ref, other_ref, left_ref, rows):
    bit = lax.axis_index(AXES) & 1
    for m in range(left_ref.shape[0]):
        left_ref[m, bit] = mine_ref[:, m * rows : (m + 1) * rows]
        left_ref[m, 1 - bit] = other_ref[:, m * rows : (m + 1) * rows]


def right_kernel(
    mine_ref, other_ref, grad_ref, error_ref, all_ref, k0_ref, k2_ref, s1_ref, s3_ref, left_ref, right_ref
):
    low_bits = lax.axis_index(AXES) & 3
    mats, rows, _ = grad_ref.shape
    gather_left(mine_ref, other_ref, left_ref, rows)
    for m in range(mats):
        high, low = split(grad_ref[m] + error_ref[m].astype(F32))
        left = left_ref[m].reshape(-1, rows)
        rank = left.shape[0]
        l_both = jnp.concatenate(split(left), 0)
        both = dot(l_both, high, ((1,), (0,))) + dot(l_both, low, ((1,), (0,)))
        total = both[:rank] + both[rank:]
        all_ref[m] = total
        right_ref[...] = total.reshape(right_ref.shape)
        k0_ref[m] = right_ref[low_bits]
        k2_ref[m] = right_ref[low_bits ^ 2]
        s1_ref[m] = right_ref[low_bits ^ 1]
        s3_ref[m] = right_ref[low_bits ^ 3]


def three(left):
    high, low = split(left)
    return jnp.concatenate([high, high, low], 0)


def three_right(right):
    high, low = split(right)
    return jnp.concatenate([high, low, high], 0)


def solve_kernel(mine_ref, other_ref, w_ref, left_ref):
    mats, _, half, rows = left_ref.shape
    rank = 2 * half
    gather_left(mine_ref, other_ref, left_ref, rows)
    left = left_ref[...].reshape(mats, rank, rows)

    def exact(x, y, contract):
        return jnp.stack(
            [
                lax.dot_general(
                    x[m], y[m], (contract, ((), ())), precision=lax.Precision.HIGHEST, preferred_element_type=F32
                )
                for m in range(mats)
            ]
        )

    gram = exact(left, left, ((1,), (1,)))
    line = lax.broadcasted_iota(jnp.int32, gram.shape, 1)
    lane = lax.broadcasted_iota(jnp.int32, gram.shape, 2)
    for k in range(rank):
        inverse = 1.0 / gram[:, k : k + 1, k : k + 1]
        row = jnp.where(lane[:, k : k + 1] == k, inverse, gram[:, k : k + 1] * inverse)
        rest = jnp.where(lane == k, 0.0, gram) - gram[:, :, k : k + 1] * row
        gram = jnp.where(line == k, row, rest)
    solved = exact(gram, left, ((1,), (0,)))
    for m in range(mats):
        w_ref[m] = three(solved[m]).T


def error_kernel(grad_ref, error_ref, w_ref, all_ref, new_ref):
    approx = dot(w_ref[0], three_right(all_ref[0]), ((1,), (0,)))
    new_ref[0] = (grad_ref[0] + error_ref[0].astype(F32) - approx).astype(BF16)


def slot_of(owners_ref, i):
    slot = jnp.int32(0)
    for j in range(owners_ref.shape[0]):
        slot += jnp.where((j < i) & (owners_ref[j] == owners_ref[i]), 1, 0).astype(jnp.int32)
    return slot


def first_kernel(
    grad_hbm, error_hbm, q_hbm, mom_hbm, mine_ref, other_ref, odd_ref,
    grad_ref, error_ref, q_ref, left_ref, sems, mom_sems,
):
    mats, rows, _ = grad_ref.shape
    rank = q_ref.shape[1]
    me = lax.axis_index(AXES)
    pairs = ((grad_hbm, grad_ref), (error_hbm, error_ref), (q_hbm, q_ref))
    copies = [
        [pltpu.make_async_copy(hbm.at[m], ref.at[m], sems.at[m, n]) for n, (hbm, ref) in enumerate(pairs)]
        for m in range(mats)
    ]
    mom_copies = [
        pltpu.make_async_copy(mom_hbm.at[slot, (2 * n + 1) ^ (me & 7)], odd_ref.at[n, slot], mom_sems.at[n, slot])
        for n in range(4)
        for slot in range(odd_ref.shape[1])
    ]
    for copy in copies[0] + copies[1] + mom_copies:
        copy.start()
    for m in range(mats):
        for copy in copies[m]:
            copy.wait()
        if m == 0:
            for copies_of in copies[2:]:
                for copy in copies_of:
                    copy.start()
        high, low = split(grad_ref[m] + error_ref[m].astype(F32))
        q_both = jnp.concatenate(split(q_ref[m]), 0)
        both = dot(q_both, high, ((1,), (1,))) + dot(q_both, low, ((1,), (1,)))
        left_ref[...] = (both[:rank] + both[rank:]).reshape(left_ref.shape)
        mine_ref[:, m * rows : (m + 1) * rows] = left_ref[me & 1]
        other_ref[:, m * rows : (m + 1) * rows] = left_ref[1 - (me & 1)]
    for copy in mom_copies:
        copy.wait()


def even_kernel(owners_ref, mom_ref, got_ref, *outs):
    me = lax.axis_index(AXES)
    for i in range(owners_ref.shape[0]):
        slot = slot_of(owners_ref, i)
        here, there = owners_ref[i] == me, owners_ref[i] == (me ^ 1)

        @pl.when(here)
        def _():
            for n, out in enumerate(outs):
                out[0, i] = mom_ref[slot, (2 * n) ^ (me & 7)]

        @pl.when(there)
        def _():
            for n, out in enumerate(outs):
                out[0, i] = got_ref[n, slot]

        @pl.when(jnp.logical_not(here | there))
        def _():
            for out in outs:
                out[0, i] = jnp.zeros(out.shape[2:], BF16)


def step_kernel(
    owners_ref, buckets_ref, rates_ref, betas_ref,
    r0_ref, r1_ref, r2_ref, r3_ref, w_ref, even_ref, odd_ref, far_ref, odd_far_ref,
    step_hbm, mom_hbm, step_ref, mom_ref, zero_ref, right_ref, update_ref, step_sems, mom_sems,
):
    me = lax.axis_index(AXES)
    mats, slots = step_ref.shape[0], mom_ref.shape[0]
    own = [owners_ref[m] == me for m in range(mats)]
    slot = [slot_of(owners_ref, m) for m in range(mats)]
    zero_ref[...] = jnp.zeros_like(zero_ref)
    for n in range(slots):
        used = jnp.bool_(False)
        for m in range(mats):
            used |= own[m] & (slot[m] == n)

        @pl.when(jnp.logical_not(used))
        def _():
            pltpu.make_async_copy(zero_ref, mom_hbm.at[n], mom_sems.at[n]).start()

    for m in range(mats):
        rate = rates_ref[buckets_ref[m]]
        beta = betas_ref[buckets_ref[m]]
        of_update, of_old = -rate * (1.0 + beta), -rate * beta * beta
        for position, ref in enumerate((r0_ref, r1_ref, r2_ref, r3_ref)):
            right_ref[position ^ (me & 3)] = ref[m]
        right = three_right(right_ref[...].reshape(-1, right_ref.shape[2]))
        update_ref[...] = dot(w_ref[m], right, ((1,), (0,))).reshape(update_ref.shape)
        for position in range(8):
            near, far = ((even_ref, far_ref), (odd_ref, odd_far_ref))[position % 2]
            piece = position ^ (me & 7)
            update = update_ref[piece]
            old = (near[position // 2, m] if position < 6 else far[0, m]).astype(F32)
            step_ref[m, piece] = (of_update * update + of_old * old).astype(BF16)

            @pl.when(own[m])
            def _():
                mom_ref[slot[m], piece] = (beta * old + update).astype(BF16)

        pltpu.make_async_copy(step_ref.at[m], step_hbm.at[m], step_sems.at[m]).start()

        @pl.when(own[m])
        def _():
            n = slot[m]
            pltpu.make_async_copy(mom_ref.at[n], mom_hbm.at[n], mom_sems.at[n]).start()

    for n in range(slots):
        pltpu.make_async_copy(zero_ref, mom_hbm.at[n], mom_sems.at[n]).wait()
    for m in range(mats):
        pltpu.make_async_copy(step_ref.at[m], step_hbm.at[m], step_sems.at[m]).wait()


def exchange(value, mask, count):
    return lax.ppermute(value, AXES, [(d, d ^ mask) for d in range(count)])


def total_over(value, bits, count):
    while bits:
        head, bits = bits[:2], bits[2:]
        masks = [1 << head[0]] if len(head) == 1 else [1 << head[0], 1 << head[1], (1 << head[0]) | (1 << head[1])]
        value = functools.reduce(jnp.add, [exchange(value, m, count) for m in masks], value)
    return value


def on_device(count, gradients, errors, q_init, owners, buckets, learn_rates, beta_values, momentum):
    grads, errs = gradients[0], errors[0]
    mats, rows, cols = grads.shape
    rank = q_init.shape[2]
    slots = momentum.shape[0]
    bits = list(range(count.bit_length() - 1))
    q_t = jnp.swapaxes(q_init, 1, 2)
    half, quarter, piece = rank // 2, rank // 4, rows // 8
    grad_spec = per_matrix((rows, cols))
    sds = jax.ShapeDtypeStruct

    def old_shape(n):
        return (n, mats, piece, cols)

    def swap(value, mask):
        return exchange(value, mask, count)

    momentum = momentum.reshape(slots, 8, piece, cols)
    mine, other, odd = pl.pallas_call(
        first_kernel,
        in_specs=[pl.BlockSpec(memory_space=pltpu.HBM)] * 4,
        out_shape=[sds((half, mats * rows), F32)] * 2 + [sds((4, slots, piece, cols), BF16)],
        scratch_shapes=[
            pltpu.VMEM((mats, rows, cols), F32),
            pltpu.VMEM((mats, rows, cols), BF16),
            pltpu.VMEM((mats, rank, cols), F32),
            pltpu.VMEM((2, half, rows), F32),
            pltpu.SemaphoreType.DMA((mats, 3)),
            pltpu.SemaphoreType.DMA((4, slots)),
        ],
        compiler_params=pltpu.CompilerParams(vmem_limit_bytes=40 * 1024 * 1024),
        name="first",
    )(*(pltpu.with_memory_space_constraint(v, pltpu.HBM) for v in (grads, errs, q_t, momentum)))

    got = swap(odd, 1)
    mine = mine + swap(other, 1)
    evens = pl.pallas_call(
        even_kernel,
        in_specs=[SMEM, VMEM, VMEM],
        out_specs=[VMEM] * 4,
        out_shape=[sds(old_shape(1), BF16)] * 4,
        compiler_params=pltpu.CompilerParams(vmem_limit_bytes=40 * 1024 * 1024),
        name="even",
    )(owners, momentum, after(got, mine))
    got = [swap(evens[n], 2 * n) for n in (1, 2, 3)]
    mine = total_over(mine, bits[3:4], count)
    mine = after(mine, *evens)
    for bit in bits[4:]:
        mine = total_over(mine, [bit], count)
    old = after(evens[0], mine) + got[0] + got[1] + got[2]
    mine = after(mine, old)
    from_other = swap(old, 1 << bits[-1])
    for bit in bits[1:3]:
        mine = total_over(mine, [bit], count)
    other = swap(mine, 1)

    right_all, keep, send2, send1, send3 = pl.pallas_call(
        right_kernel,
        in_specs=[VMEM] * 4,
        out_specs=[VMEM] * 5,
        out_shape=[sds((mats, rank, cols), F32)] + [sds((mats, quarter, cols), F32)] * 4,
        scratch_shapes=[pltpu.VMEM((mats, 2, half, rows), F32), pltpu.VMEM((4, quarter, cols), F32)],
        compiler_params=pltpu.CompilerParams(vmem_limit_bytes=40 * 1024 * 1024),
        name="right",
    )(mine, other, grads, errs)

    w = pl.pallas_call(
        solve_kernel,
        grid=(1,),
        in_specs=[whole((half, mats * rows))] * 2,
        out_specs=whole((mats, rows, 3 * rank)),
        out_shape=sds((mats, rows, 3 * rank), BF16),
        scratch_shapes=[pltpu.VMEM((mats, 2, half, rows), F32)],
        compiler_params=params(),
        cost_estimate=cost(1),
        name="solve",
    )(mine, other)

    got = swap(send1, 1), swap(send3, 1)
    r0, send2 = keep + got[0], send2 + got[1]
    old = after(old, r0, send2) + from_other
    for bit in reversed(bits[4:-1]):
        old = old + swap(old, 1 << bit)
    send2 = after(send2, old)
    from_other = swap(old, 1 << bits[3])
    r0 = r0 + swap(send2, 2)
    r0 = total_over(r0, bits[2:3], count)
    old = after(old, r0, w) + from_other
    r0 = after(r0, old)
    near = [swap(old, 2), swap(old, 4)]
    for n, bit in enumerate(bits[3:]):
        r0 = total_over(r0, [bit], count)
        if n == 0:
            near = [after(value, r0) for value in near]
            r0 = after(r0, *near)
    far = swap(near[0], 4)
    new_errors = pl.pallas_call(
        error_kernel,
        grid=(mats,),
        in_specs=[grad_spec, grad_spec, per_matrix((rows, 3 * rank)), per_matrix((rank, cols))],
        out_specs=grad_spec,
        out_shape=sds((mats, rows, cols), BF16),
        compiler_params=params(),
        cost_estimate=cost(12),
        name="errors",
    )(grads, errs, after(w, *near), right_all)
    r0 = after(r0, new_errors)
    r1, r2 = swap(r0, 1), swap(r0, 2)
    evens = jnp.concatenate([old] + near)
    odds = swap(evens, 1)
    r3 = swap(r2, 1)
    far = after(far, r0)
    odd_far = swap(after(far, r2), 1)

    pieces = (8, piece, cols)
    steps, new_mom = pl.pallas_call(
        step_kernel,
        in_specs=[SMEM] * 4 + [VMEM] * 9,
        out_specs=[ANY] * 2,
        out_shape=[sds((mats,) + pieces, BF16), sds((slots,) + pieces, BF16)],
        scratch_shapes=[
            pltpu.VMEM((mats,) + pieces, BF16),
            pltpu.VMEM((slots,) + pieces, BF16),
            pltpu.VMEM(pieces, BF16),
            pltpu.VMEM((4, quarter, cols), F32),
            pltpu.VMEM(pieces, F32),
            pltpu.SemaphoreType.DMA((mats,)),
            pltpu.SemaphoreType.DMA((slots,)),
        ],
        compiler_params=pltpu.CompilerParams(vmem_limit_bytes=40 * 1024 * 1024),
        name="step",
    )(owners, buckets, learn_rates, beta_values, r0, r1, r2, r3, w, evens, odds, far, odd_far)
    return (new_errors[None], steps.reshape(1, mats, rows, cols), new_mom.reshape(slots, rows, cols))


def solution(mesh):
    count = mesh.shape["dp"] * mesh.shape["group"]
    rep = P(AXES, None, None, None)
    return jax.shard_map(
        functools.partial(on_device, count),
        mesh=mesh,
        in_specs=(rep, rep, P(), P(), P(), P(), P(), P(AXES, None, None)),
        out_specs=(rep, rep, P(AXES, None, None)),
        check_vma=False,
    )
```

```python
import functools

import jax
import jax.numpy as jnp
from jax import lax
from jax.experimental import pallas as pl
from jax.experimental.pallas import tpu as pltpu
from jax.sharding import PartitionSpec as P

AXES = ("dp", "group")
F32 = jnp.float32
BF16 = jnp.bfloat16
SMEM = pl.BlockSpec(memory_space=pltpu.SMEM)
VMEM = pl.BlockSpec(memory_space=pltpu.VMEM)
ANY = pl.BlockSpec(memory_space=pl.ANY)


def whole(shape):
    return pl.BlockSpec(shape, lambda i: (0,) * len(shape))


def per_matrix(shape):
    return pl.BlockSpec((1,) + shape, lambda i: (i,) + (0,) * len(shape))


def split(value):
    high = value.astype(BF16)
    return high, (value - high.astype(F32)).astype(BF16)


def dot(left, right, dims):
    return lax.dot_general(left, right, (dims, ((), ())), preferred_element_type=F32)


def params(mebibytes=40):
    return pltpu.CompilerParams(dimension_semantics=("arbitrary",), vmem_limit_bytes=mebibytes * 1024 * 1024)


def cost(mebibytes):
    return pl.CostEstimate(flops=0, transcendentals=0, bytes_accessed=mebibytes * 1024 * 1024)


def after(value, *others):
    return lax.optimization_barrier((value,) + others)[0]


def gather_left(mine_ref, other_ref, left_ref, rows):
    bit = lax.axis_index(AXES) & 1
    for m in range(left_ref.shape[0]):
        left_ref[m, bit] = mine_ref[:, m * rows : (m + 1) * rows]
        left_ref[m, 1 - bit] = other_ref[:, m * rows : (m + 1) * rows]


def right_kernel(
    mine_ref, other_ref, grad_ref, error_ref, all_ref, k0_ref, k2_ref, s1_ref, s3_ref, left_ref, right_ref
):
    low_bits = lax.axis_index(AXES) & 3
    mats, rows, _ = grad_ref.shape
    gather_left(mine_ref, other_ref, left_ref, rows)
    for m in range(mats):
        high, low = split(grad_ref[m] + error_ref[m].astype(F32))
        left = left_ref[m].reshape(-1, rows)
        rank = left.shape[0]
        l_both = jnp.concatenate(split(left), 0)
        both = dot(l_both, high, ((1,), (0,))) + dot(l_both, low, ((1,), (0,)))
        total = both[:rank] + both[rank:]
        all_ref[m] = total
        right_ref[...] = total.reshape(right_ref.shape)
        k0_ref[m] = right_ref[low_bits]
        k2_ref[m] = right_ref[low_bits ^ 2]
        s1_ref[m] = right_ref[low_bits ^ 1]
        s3_ref[m] = right_ref[low_bits ^ 3]


def three(left):
    high, low = split(left)
    return jnp.concatenate([high, high, low], 0)


def three_right(right):
    high, low = split(right)
    return jnp.concatenate([high, low, high], 0)


def solve_kernel(mine_ref, other_ref, w_ref, left_ref):
    mats, _, half, rows = left_ref.shape
    rank = 2 * half
    gather_left(mine_ref, other_ref, left_ref, rows)
    left = left_ref[...].reshape(mats, rank, rows)

    def exact(x, y, contract):
        return jnp.stack(
            [
                lax.dot_general(
                    x[m], y[m], (contract, ((), ())), precision=lax.Precision.HIGHEST, preferred_element_type=F32
                )
                for m in range(mats)
            ]
        )

    gram = exact(left, left, ((1,), (1,)))
    line = lax.broadcasted_iota(jnp.int32, gram.shape, 1)
    lane = lax.broadcasted_iota(jnp.int32, gram.shape, 2)
    for k in range(rank):
        inverse = 1.0 / gram[:, k : k + 1, k : k + 1]
        row = jnp.where(lane[:, k : k + 1] == k, inverse, gram[:, k : k + 1] * inverse)
        rest = jnp.where(lane == k, 0.0, gram) - gram[:, :, k : k + 1] * row
        gram = jnp.where(line == k, row, rest)
    solved = exact(gram, left, ((1,), (0,)))
    for m in range(mats):
        w_ref[m] = three(solved[m]).T


def error_kernel(grad_ref, error_ref, w_ref, all_ref, new_ref):
    approx = dot(w_ref[0], three_right(all_ref[0]), ((1,), (0,)))
    new_ref[0] = (grad_ref[0] + error_ref[0].astype(F32) - approx).astype(BF16)


def slot_of(owners_ref, i):
    slot = jnp.int32(0)
    for j in range(owners_ref.shape[0]):
        slot += jnp.where((j < i) & (owners_ref[j] == owners_ref[i]), 1, 0).astype(jnp.int32)
    return slot


def first_kernel(
    grad_hbm, error_hbm, q_hbm, mom_hbm, mine_ref, other_ref, odd_ref, grad_ref, error_ref,
    q_ref, left_ref, sems, mom_sems,
):
    mats, rows, _ = grad_ref.shape
    rank = q_ref.shape[1]
    me = lax.axis_index(AXES)
    pairs = ((grad_hbm, grad_ref), (error_hbm, error_ref), (q_hbm, q_ref))
    copies = [
        [pltpu.make_async_copy(hbm.at[m], ref.at[m], sems.at[m, n]) for n, (hbm, ref) in enumerate(pairs)]
        for m in range(mats)
    ]
    mom_copies = [
        pltpu.make_async_copy(mom_hbm.at[slot, (2 * n + 1) ^ (me & 7)], odd_ref.at[n, slot], mom_sems.at[n, slot])
        for n in range(4)
        for slot in range(odd_ref.shape[1])
    ]
    for copy in copies[0] + copies[1] + mom_copies:
        copy.start()
    for m in range(mats):
        for copy in copies[m]:
            copy.wait()
        if m == 0:
            for copies_of in copies[2:]:
                for copy in copies_of:
                    copy.start()
        high, low = split(grad_ref[m] + error_ref[m].astype(F32))
        q_both = jnp.concatenate(split(q_ref[m]), 0)
        both = dot(q_both, high, ((1,), (1,))) + dot(q_both, low, ((1,), (1,)))
        left_ref[...] = (both[:rank] + both[rank:]).reshape(left_ref.shape)
        mine_ref[:, m * rows : (m + 1) * rows] = left_ref[me & 1]
        other_ref[:, m * rows : (m + 1) * rows] = left_ref[1 - (me & 1)]
    for copy in mom_copies:
        copy.wait()


def even_kernel(owners_ref, mom_ref, got_ref, *outs):
    me = lax.axis_index(AXES)
    for i in range(owners_ref.shape[0]):
        slot = slot_of(owners_ref, i)
        here, there = owners_ref[i] == me, owners_ref[i] == (me ^ 1)

        @pl.when(here)
        def _():
            for n, out in enumerate(outs):
                out[0, i] = mom_ref[slot, (2 * n) ^ (me & 7)]

        @pl.when(there)
        def _():
            for n, out in enumerate(outs):
                out[0, i] = got_ref[n, slot]

        @pl.when(jnp.logical_not(here | there))
        def _():
            for out in outs:
                out[0, i] = jnp.zeros(out.shape[2:], BF16)


def step_kernel(
    owners_ref, buckets_ref, rates_ref, betas_ref,
    r0_ref, r1_ref, r2_ref, r3_ref, w_ref, even_ref, odd_ref, far_ref, odd_far_ref,
    step_hbm, mom_hbm, step_ref, mom_ref, zero_ref, right_ref, update_ref, step_sems, mom_sems,
):
    me = lax.axis_index(AXES)
    mats, slots = step_ref.shape[0], mom_ref.shape[0]
    own = [owners_ref[m] == me for m in range(mats)]
    slot = [slot_of(owners_ref, m) for m in range(mats)]
    zero_ref[...] = jnp.zeros_like(zero_ref)
    for n in range(slots):
        used = jnp.bool_(False)
        for m in range(mats):
            used |= own[m] & (slot[m] == n)

        @pl.when(jnp.logical_not(used))
        def _():
            pltpu.make_async_copy(zero_ref, mom_hbm.at[n], mom_sems.at[n]).start()

    for m in range(mats):
        rate = rates_ref[buckets_ref[m]]
        beta = betas_ref[buckets_ref[m]]
        of_update, of_old = -rate * (1.0 + beta), -rate * beta * beta
        for position, ref in enumerate((r0_ref, r1_ref, r2_ref, r3_ref)):
            right_ref[position ^ (me & 3)] = ref[m]
        right = three_right(right_ref[...].reshape(-1, right_ref.shape[2]))
        update_ref[...] = dot(w_ref[m], right, ((1,), (0,))).reshape(update_ref.shape)
        for position in range(8):
            near, far = ((even_ref, far_ref), (odd_ref, odd_far_ref))[position % 2]
            piece = position ^ (me & 7)
            update = update_ref[piece]
            old = (near[position // 2, m] if position < 6 else far[0, m]).astype(F32)
            step_ref[m, piece] = (of_update * update + of_old * old).astype(BF16)

            @pl.when(own[m])
            def _():
                mom_ref[slot[m], piece] = (beta * old + update).astype(BF16)

        pltpu.make_async_copy(step_ref.at[m], step_hbm.at[m], step_sems.at[m]).start()

        @pl.when(own[m])
        def _():
            n = slot[m]
            pltpu.make_async_copy(mom_ref.at[n], mom_hbm.at[n], mom_sems.at[n]).start()

    for n in range(slots):
        pltpu.make_async_copy(zero_ref, mom_hbm.at[n], mom_sems.at[n]).wait()
    for m in range(mats):
        pltpu.make_async_copy(step_ref.at[m], step_hbm.at[m], step_sems.at[m]).wait()


def exchange(value, mask, count):
    return lax.ppermute(value, AXES, [(d, d ^ mask) for d in range(count)])


def total_over(value, bits, count):
    while bits:
        head, bits = bits[:2], bits[2:]
        masks = [1 << head[0]] if len(head) == 1 else [1 << head[0], 1 << head[1], (1 << head[0]) | (1 << head[1])]
        value = functools.reduce(jnp.add, [exchange(value, m, count) for m in masks], value)
    return value


def on_device(count, gradients, errors, q_init, owners, buckets, learn_rates, beta_values, momentum):
    grads, errs = gradients[0], errors[0]
    mats, rows, cols = grads.shape
    rank = q_init.shape[2]
    slots = momentum.shape[0]
    bits = list(range(count.bit_length() - 1))
    q_t = jnp.swapaxes(q_init, 1, 2)
    half, quarter, piece = rank // 2, rank // 4, rows // 8
    grad_spec = per_matrix((rows, cols))
    sds = jax.ShapeDtypeStruct

    def old_shape(n):
        return (n, mats, piece, cols)

    def swap(value, mask):
        return exchange(value, mask, count)

    momentum = momentum.reshape(slots, 8, piece, cols)
    mine, other, odd, grads, errs = pl.pallas_call(
        first_kernel,
        in_specs=[pl.BlockSpec(memory_space=pltpu.HBM)] * 4,
        out_specs=[VMEM] * 5,
        out_shape=[sds((half, mats * rows), F32)] * 2
        + [sds((4, slots, piece, cols), BF16), sds((mats, rows, cols), F32), sds((mats, rows, cols), BF16)],
        scratch_shapes=[
            pltpu.VMEM((mats, rank, cols), F32),
            pltpu.VMEM((2, half, rows), F32),
            pltpu.SemaphoreType.DMA((mats, 3)),
            pltpu.SemaphoreType.DMA((4, slots)),
        ],
        compiler_params=pltpu.CompilerParams(vmem_limit_bytes=40 * 1024 * 1024),
        name="first",
    )(*(pltpu.with_memory_space_constraint(v, pltpu.HBM) for v in (grads, errs, q_t, momentum)))

    got = swap(odd, 1)
    mine = mine + swap(other, 1)
    evens = pl.pallas_call(
        even_kernel,
        in_specs=[SMEM, VMEM, VMEM],
        out_specs=[VMEM] * 4,
        out_shape=[sds(old_shape(1), BF16)] * 4,
        compiler_params=pltpu.CompilerParams(vmem_limit_bytes=40 * 1024 * 1024),
        name="even",
    )(owners, momentum, after(got, mine))
    got = [swap(evens[n], 2 * n) for n in (1, 2, 3)]
    mine = total_over(mine, bits[3:4], count)
    mine = after(mine, *evens)
    for bit in bits[4:]:
        mine = total_over(mine, [bit], count)
    old = after(evens[0], mine) + got[0] + got[1] + got[2]
    mine = after(mine, old)
    from_other = swap(old, 1 << bits[-1])
    for bit in bits[1:3]:
        mine = total_over(mine, [bit], count)
    other = swap(mine, 1)

    right_all, keep, send2, send1, send3 = pl.pallas_call(
        right_kernel,
        in_specs=[VMEM] * 4,
        out_specs=[VMEM] * 5,
        out_shape=[sds((mats, rank, cols), F32)] + [sds((mats, quarter, cols), F32)] * 4,
        scratch_shapes=[pltpu.VMEM((mats, 2, half, rows), F32), pltpu.VMEM((4, quarter, cols), F32)],
        compiler_params=pltpu.CompilerParams(vmem_limit_bytes=40 * 1024 * 1024),
        name="right",
    )(mine, other, grads, errs)

    w = pl.pallas_call(
        solve_kernel,
        grid=(1,),
        in_specs=[whole((half, mats * rows))] * 2,
        out_specs=whole((mats, rows, 3 * rank)),
        out_shape=sds((mats, rows, 3 * rank), BF16),
        scratch_shapes=[pltpu.VMEM((mats, 2, half, rows), F32)],
        compiler_params=params(),
        cost_estimate=cost(1),
        name="solve",
    )(mine, other)

    got = swap(send1, 1), swap(send3, 1)
    r0, send2 = keep + got[0], send2 + got[1]
    old = after(old, r0, send2) + from_other
    for bit in reversed(bits[4:-1]):
        old = old + swap(old, 1 << bit)
    send2 = after(send2, old)
    from_other = swap(old, 1 << bits[3])
    r0 = r0 + swap(send2, 2)
    r0 = total_over(r0, bits[2:3], count)
    old = after(old, r0, w) + from_other
    r0 = after(r0, old)
    near = [swap(old, 2), swap(old, 4)]
    for n, bit in enumerate(bits[3:]):
        r0 = total_over(r0, [bit], count)
        if n == 0:
            near = [after(value, r0) for value in near]
            r0 = after(r0, *near)
    far = swap(near[0], 4)
    new_errors = pl.pallas_call(
        error_kernel,
        grid=(mats,),
        in_specs=[grad_spec, grad_spec, per_matrix((rows, 3 * rank)), per_matrix((rank, cols))],
        out_specs=grad_spec,
        out_shape=sds((mats, rows, cols), BF16),
        compiler_params=params(),
        cost_estimate=cost(12),
        name="errors",
    )(grads, errs, after(w, *near), right_all)
    r0 = after(r0, new_errors)
    r1, r2 = swap(r0, 1), swap(r0, 2)
    evens = jnp.concatenate([old] + near)
    odds = swap(evens, 1)
    r3 = swap(r2, 1)
    far = after(far, r0)
    odd_far = swap(after(far, r2), 1)

    pieces = (8, piece, cols)
    steps, new_mom = pl.pallas_call(
        step_kernel,
        in_specs=[SMEM] * 4 + [VMEM] * 9,
        out_specs=[ANY] * 2,
        out_shape=[sds((mats,) + pieces, BF16), sds((slots,) + pieces, BF16)],
        scratch_shapes=[
            pltpu.VMEM((mats,) + pieces, BF16),
            pltpu.VMEM((slots,) + pieces, BF16),
            pltpu.VMEM(pieces, BF16),
            pltpu.VMEM((4, quarter, cols), F32),
            pltpu.VMEM(pieces, F32),
            pltpu.SemaphoreType.DMA((mats,)),
            pltpu.SemaphoreType.DMA((slots,)),
        ],
        compiler_params=pltpu.CompilerParams(vmem_limit_bytes=40 * 1024 * 1024),
        name="step",
    )(owners, buckets, learn_rates, beta_values, r0, r1, r2, r3, w, evens, odds, far, odd_far)
    return (new_errors[None], steps.reshape(1, mats, rows, cols), new_mom.reshape(slots, rows, cols))


def solution(mesh):
    count = mesh.shape["dp"] * mesh.shape["group"]
    rep = P(AXES, None, None, None)
    return jax.shard_map(
        functools.partial(on_device, count),
        mesh=mesh,
        in_specs=(rep, rep, P(), P(), P(), P(), P(), P(AXES, None, None)),
        out_specs=(rep, rep, P(AXES, None, None)),
        check_vma=False,
    )
```
